512 devices in a mesh: dp: 8 (over y, core), mp: 64 (over x, z).
Axes of the slice: x: 4, y: 4, z: 16, core: 2. Of those that a mesh axis runs over, the one named last changes fastest.
Arguments:
- query: bfloat16 [2048, 4096], P('dp', 'mp'), may hold values from -0.75 to 0.75
- kv_cache: bfloat16 [16384, 8192], P('dp', 'mp'), may hold values from -4 to 4, as said below
- out_grad: bfloat16 [2048, 4096], P('dp', 'mp'), may hold values from -384 to 384
- source_lengths: int32 [8, 8], P('dp'), may hold values from 1 to 512, 2048 in all within a row
- target_lengths: int32 [8, 8], P('dp'), may hold values from 1 to 64, 256 in all within a row
- low_rank: bfloat16 [16384, 32], P(('dp', 'mp')), may hold values from -0.125 to 0.125
- adapter_up_matrix: bfloat16 [32, 4096], replicated, may hold values from -0.09375 to 0.09375
Outputs:
- query_grad: bfloat16 [2048, 4096], P('dp', 'mp')
- key_gradient: bfloat16 [16384, 4096], P(('dp', 'mp'))
- value_grad: bfloat16 [16384, 4096], P(('dp', 'mp'))
- low_rank_gradient: float32 [16384, 32], P(('dp', 'mp'))
- adapter_up_gradient: float32 [4096, 32], P(('dp', 'mp'))
The draws below stay inside these ranges and needn't reach their ends.
Inputs may be any that keep to these rules, and one draw needn't show every extreme that they name: `source_lengths`: each row sums to 2048; its largest entry is exactly 512. `target_lengths`: each row sums to 256; its largest entry is exactly 64. `kv_cache`: the key columns lie within -0.75 to 0.75.
All inputs are finite; a program needn't handle non-finite values.
Results may differ from the reference program's by a relative error of at most 0.0053.
Values may be sent and summed in bfloat16 or wider, within the bound.
A program may use at most 64 MiB of HBM per device.

```python
import math
import jax
import jax.numpy as jnp
import numpy as np
from jax import lax

HS = 64
HEADS = 64
D = 4096
ADAPTER_RANK = 16
NDOC = 8
TQ = 256
PACKS = 8
S = 2048


def scaled_heads(key, rows):
    first, second = jax.random.split(key)
    scales = jnp.exp(jax.random.uniform(first, (rows, HEADS, 1), jnp.float32, math.log(0.25), 0.0))
    base = jnp.clip(0.5 * jax.random.normal(second, (rows, HEADS, HS), jnp.float32), -0.75, 0.75)
    return base * scales


def draw_query(key, part):
    rows = PACKS * TQ
    return scaled_heads(jax.random.fold_in(key, 11), rows).reshape(rows, HEADS * HS).astype(jnp.bfloat16)


def draw_kv_cache(key, part):
    rows = PACKS * S
    keys_part = scaled_heads(jax.random.fold_in(key, 23), rows)
    values_part = jnp.clip(jax.random.normal(jax.random.fold_in(key, 37), (rows, HEADS, HS), jnp.float32), -4.0, 4.0)
    both = jnp.stack([keys_part, values_part], axis=2)
    return both.reshape(rows, 2 * HEADS * HS).astype(jnp.bfloat16)


def level_of(key, dims, pieces, smallest, largest):
    level = 1.0
    for dim, blocks in pieces:
        heights = jax.random.uniform(jax.random.fold_in(jax.random.fold_in(key, 6), dim), (blocks,), jnp.float32, smallest / len(pieces), largest / len(pieces))
        level = level * jnp.repeat(jnp.exp(heights), dims[dim] // blocks).reshape((-1,) + (1,) * (len(dims) - 1 - dim))
    return level


def profile(amount, total, most, skew):
    portions = [(1 << 20) // math.isqrt(rank ** skew) + 1 for rank in range(2, amount + 1)]
    surplus, holding = total - most - (amount - 1), [1] * (amount - 1)
    while surplus > 0:
        free = [i for i in range(amount - 1) if holding[i] < most]
        whole, remaining = sum([portions[i] for i in free]), surplus
        for i in free:
            more = min(most - holding[i], max(1, remaining * portions[i] // whole), surplus)
            holding[i] = holding[i] + more
            surplus = surplus - more
    return np.array([most] + holding)


def uneven_parts(own_key, number_of, total, reach, skew):
    if number_of == 2:
        one = jax.random.randint(own_key, (), max(1, total - reach), min(reach, total - 1) + 1)
        return jnp.stack([one, total - one])
    tallies = jnp.asarray(profile(number_of, total, reach, skew), jnp.int32)
    couples = (number_of - 1) // 2
    giver, taker = tallies[1:1 + 2 * couples:2], tallies[2:2 + 2 * couples:2]
    margin = jnp.minimum(giver - 1, reach - taker)
    passed = jax.random.randint(jax.random.fold_in(own_key, 1), (couples,), 0, 1 << 20) % (margin + 1)
    tallies = tallies.at[1:1 + 2 * couples:2].set(giver - passed).at[2:2 + 2 * couples:2].set(taker + passed)
    return tallies[jax.random.permutation(jax.random.fold_in(own_key, 2), number_of)]


def gaussian(rng, extent, deviation, limit, cuts=(), kind=jnp.bfloat16):
    level = level_of(rng, extent, cuts, -0.22, 0.18) if cuts else 1.0
    drawn = jax.random.normal(rng, extent, jnp.float32) * deviation * level
    return jnp.minimum(jnp.maximum(drawn, -limit), limit).astype(kind)


def setup_inputs(seed: int = 0) -> dict:
    seeds = jax.random.split(jax.random.key(seed), 8)
    query = draw_query(jax.random.fold_in(seeds[7], 71), 0)
    kv_cache = draw_kv_cache(jax.random.fold_in(seeds[7], 71), 0)
    out_grad = gaussian(seeds[2], (PACKS * TQ, D), 64.0, 384.0, ((0, 8), (1, 64)))
    source_lengths = jax.vmap(lambda own: uneven_parts(own, NDOC, S, S // 4, 2))(jax.random.split(seeds[3], PACKS)).reshape((PACKS, NDOC)).astype(jnp.int32)
    target_lengths = jax.vmap(lambda own: uneven_parts(own, NDOC, TQ, TQ // 4, 2))(jax.random.split(seeds[4], PACKS)).reshape((PACKS, NDOC)).astype(jnp.int32)
    low_rank = gaussian(seeds[5], (PACKS * S, 2 * ADAPTER_RANK), 0.02, 0.125, ((0, 512),))
    adapter_up_matrix = gaussian(seeds[6], (2 * ADAPTER_RANK, D), D ** -0.5, 0.09375)
    return dict(query=query, kv_cache=kv_cache, out_grad=out_grad, source_lengths=source_lengths, target_lengths=target_lengths, low_rank=low_rank, adapter_up_matrix=adapter_up_matrix)


adapter_factor = 2.0


def doc_index(lengths, count):
    ends = jnp.cumsum(lengths.astype(jnp.int32)).astype(jnp.int32)
    position = jnp.arange(count, dtype=jnp.int32)
    return jnp.sum((position[:, None] >= ends[None, :]).astype(jnp.int32), axis=1)


def reference(query, kv_cache, out_grad, source_lengths, target_lengths, low_rank, adapter_up_matrix):
    query_parts = []
    key_parts = []
    value_parts = []
    for pack in range(PACKS):
        query_pack = query[pack * TQ:(pack + 1) * TQ].reshape(TQ, HEADS, HS).transpose(1, 0, 2)
        grad_pack = out_grad[pack * TQ:(pack + 1) * TQ].reshape(TQ, HEADS, HS).transpose(1, 0, 2)
        both_pack = kv_cache[pack * S:(pack + 1) * S].reshape(S, HEADS, 2, HS)
        key_pack = both_pack[:, :, 0, :].transpose(1, 0, 2)
        value_pack = both_pack[:, :, 1, :].transpose(1, 0, 2)
        allowed = doc_index(target_lengths[pack], TQ)[:, None] == doc_index(source_lengths[pack], S)[None, :]

        def one_head(operands):
            query_head, key_head, value_head, grad_head = operands
            scores = jnp.dot(query_head, key_head.T, preferred_element_type=jnp.float32)
            expo = jnp.where(allowed, jnp.exp(scores), jnp.zeros_like(scores))
            total = jnp.sum(expo, axis=1)
            dprob = jnp.dot(grad_head, value_head.T, preferred_element_type=jnp.float32)
            delta = jnp.sum(expo * dprob, axis=1) / total
            prob = expo / total[:, None]
            prob_low = prob.astype(jnp.bfloat16)
            dscore = (prob * (dprob - delta[:, None])).astype(jnp.bfloat16)
            head_query = jnp.dot(dscore, key_head, preferred_element_type=jnp.float32).astype(jnp.bfloat16)
            head_key = jnp.dot(dscore.T, query_head, preferred_element_type=jnp.float32).astype(jnp.bfloat16)
            head_value = jnp.dot(prob_low.T, grad_head, preferred_element_type=jnp.float32).astype(jnp.bfloat16)
            return head_query, head_key, head_value

        heads_query, heads_key, heads_value = lax.map(one_head, (query_pack, key_pack, value_pack, grad_pack))
        query_parts.append(heads_query.transpose(1, 0, 2).reshape(TQ, HEADS * HS))
        key_parts.append(heads_key.transpose(1, 0, 2).reshape(S, HEADS * HS))
        value_parts.append(heads_value.transpose(1, 0, 2).reshape(S, HEADS * HS))
    query_grad = jnp.concatenate(query_parts, axis=0)
    key_gradient = jnp.concatenate(key_parts, axis=0)
    value_grad = jnp.concatenate(value_parts, axis=0)
    low_rank_gradient = adapter_factor * jnp.concatenate(
        [jnp.dot(key_gradient, adapter_up_matrix[:ADAPTER_RANK].T, preferred_element_type=jnp.float32),
         jnp.dot(value_grad, adapter_up_matrix[ADAPTER_RANK:].T, preferred_element_type=jnp.float32)], axis=1)
    adapter_up_gradient = adapter_factor * jnp.concatenate(
        [jnp.dot(key_gradient.T, low_rank[:, :ADAPTER_RANK], preferred_element_type=jnp.float32),
         jnp.dot(value_grad.T, low_rank[:, ADAPTER_RANK:], preferred_element_type=jnp.float32)], axis=1)
    return query_grad, key_gradient, value_grad, low_rank_gradient, adapter_up_gradient
```

```python
import functools

import jax
import jax.numpy as jnp
from jax import lax
from jax.experimental import pallas as pl
from jax.experimental.pallas import tpu as pltpu
from jax.sharding import PartitionSpec as P

HS = 64
XS, ZS = 4, 16
MP = XS * ZS
DP = 8
NDOC = 8
TQ = 256
S = 2048
OWN = S // MP
RANK2 = 32
ROWS = 256
ADAPTER_FACTOR = 2.0
MESH = pl.DeviceIdType.MESH
F32 = jnp.float32
BF16 = jnp.bfloat16
NT = (((1,), (1,)), ((), ()))
TN = (((0,), (0,)), ((), ()))


def fold8(x):
    return jnp.sum(x.reshape(x.shape[0] // 8, 8, x.shape[1]), axis=0)


def far_first(u):
    half = (u + 1) // 2
    return jnp.where(u % 2 == 1, 8 - half, 8 + half) % ZS


def exchange_kernel(
    q_hbm, kv_hbm, g_hbm, slen, tlen, lr_hbm,
    recv, adapter_recv, qg_out,
    q_v, kv_v, g_v, lr_v, w1, expo_s, dprob_s, ds_s, msg, lr_all, lr_full, adapter_send,
    in_sem, send_sem, recv_sem, lrz_send, lrz_recv, lrx_send, lrx_recv, ad_send, ad_recv, own_sem,
):
    p = lax.axis_index("dp")
    m = lax.axis_index("mp")
    x = m // ZS
    z = m % ZS
    ga = m // 8
    gb = m % 8
    self_adapter = jnp.logical_and(p == ga, gb == ga)

    barrier = pltpu.get_barrier_semaphore()

    def greet(s, _):
        pl.semaphore_signal(barrier, inc=1, device_id=(p, (m + s) % MP), device_id_type=MESH)
        return 0

    lax.fori_loop(1, MP, greet, 0)
    src_head = 8 * p + m // 8
    for j in range(DP):
        not_me = jnp.logical_not(jnp.logical_and(p == j, src_head == m))

        @pl.when(not_me)
        def _():
            pl.semaphore_signal(barrier, inc=1, device_id=(j, src_head), device_id_type=MESH)

    loads = [
        pltpu.make_async_copy(a, b, in_sem.at[i])
        for i, (a, b) in enumerate(((q_hbm, q_v), (g_hbm, g_v), (kv_hbm, kv_v), (lr_hbm, lr_v)))
    ]
    for c in loads:
        c.start()

    col = lax.broadcasted_iota(jnp.int32, (8, TQ), 1)
    lo = jnp.zeros((8, TQ), jnp.int32)
    hi = jnp.zeros((8, TQ), jnp.int32)
    start = jnp.int32(0)
    for k in range(NDOC):
        width = slen[0, k]
        hi = hi + jnp.where(col >= start, width, 0)
        start = start + tlen[0, k]
        lo = lo + jnp.where(col >= start, width, 0)
    lo = lo[0:1]
    hi = hi[0:1]

    loads[0].wait()
    loads[1].wait()
    zero = jnp.zeros((TQ, HS), F32)
    w1[0:TQ, :] = jnp.concatenate([q_v[...].astype(F32), zero], axis=1).astype(BF16)
    w1[TQ : 2 * TQ, :] = jnp.concatenate([zero, g_v[...].astype(F32)], axis=1).astype(BF16)
    loads[2].wait()

    row = lax.broadcasted_iota(jnp.int32, (ROWS, TQ), 0)

    def first(i, carry):
        total, weighted = carry
        base = pl.multiple_of(i * ROWS, ROWS)
        both = lax.dot_general(kv_v[pl.ds(base, ROWS), :], w1[...], NT, preferred_element_type=F32)
        dprob = both[:, TQ:]
        pos = row + base
        allowed = jnp.logical_and(pos >= lo, pos < hi)
        expo = jnp.where(allowed, jnp.exp(both[:, :TQ]), 0.0)
        expo_s[pl.ds(base, ROWS), :] = expo
        dprob_s[pl.ds(base, ROWS), :] = dprob
        return total + fold8(expo), weighted + fold8(expo * dprob)

    zeros = jnp.zeros((8, TQ), F32)
    total, weighted = lax.fori_loop(0, S // ROWS, first, (zeros, zeros))
    total = jnp.sum(total, axis=0, keepdims=True)
    delta = jnp.sum(weighted, axis=0, keepdims=True) / total
    scale = 1.0 / total

    def second(i, _):
        base = pl.multiple_of(i * ROWS, ROWS)
        prob = expo_s[pl.ds(base, ROWS), :] * scale
        ds = (prob * (dprob_s[pl.ds(base, ROWS), :] - delta)).astype(BF16)
        ds_s[pl.ds(base, ROWS), :] = ds
        both = jnp.concatenate([ds, prob.astype(BF16)], axis=1)
        grads = jnp.dot(both, w1[...], preferred_element_type=F32).astype(BF16)
        msg[pl.ds(pl.multiple_of(i * (ROWS // OWN), ROWS // OWN), ROWS // OWN)] = grads.reshape(
            ROWS // OWN, OWN, 2 * HS
        )
        return 0

    lax.fori_loop(0, S // ROWS, second, 0)

    loads[3].wait()
    lr = lr_v[...].astype(F32)
    packed = jnp.concatenate([lr[8 * j : 8 * j + 8] for j in range(4)], axis=1).astype(BF16)
    lr_all[pl.ds(m, 1)] = packed.reshape(1, 8, 4 * RANK2)

    pl.semaphore_wait(barrier, MP - 1 + DP - self_adapter.astype(jnp.int32))

    def lr_z(s, _):
        peer = x * ZS + (z + s) % ZS
        pltpu.make_async_remote_copy(
            src_ref=lr_all.at[m], dst_ref=lr_all.at[m], send_sem=lrz_send, recv_sem=lrz_recv,
            device_id=(p, peer), device_id_type=MESH,
        ).start()
        return 0

    lax.fori_loop(1, ZS, lr_z, 0)

    def send(s, _):
        peer = ((x + (s + 1) % XS) % XS) * ZS + (z + far_first(s // XS)) % ZS
        pltpu.make_async_remote_copy(
            src_ref=msg.at[peer], dst_ref=recv.at[m], send_sem=send_sem, recv_sem=recv_sem,
            device_id=(p, peer), device_id_type=MESH,
        ).start()
        return 0

    own = pltpu.make_async_copy(msg.at[m], recv.at[m], own_sem.at[0])
    own.start()
    lax.fori_loop(0, 24, send, 0)

    qg_out[...] = lax.dot_general(ds_s[...], kv_v[...], TN, preferred_element_type=F32)[:, :HS].astype(BF16)

    def wait_bytes(ref, count, sem):
        pltpu.make_async_copy(ref.at[pl.ds(0, count)], ref.at[pl.ds(0, count)], sem).wait()

    wait_bytes(lr_all, ZS - 1, lrz_recv)
    mine = lr_all.at[pl.ds(pl.multiple_of(x * ZS, ZS), ZS)]
    for j in range(1, XS):
        pltpu.make_async_remote_copy(
            src_ref=mine, dst_ref=mine, send_sem=lrx_send, recv_sem=lrx_recv,
            device_id=(p, ((x + j) % XS) * ZS + z), device_id_type=MESH,
        ).start()

    lax.fori_loop(24, 44, send, 0)

    wait_bytes(lr_all, ZS * (XS - 1), lrx_recv)
    gathered = lr_all[...].astype(F32)
    for j in range(4):
        lr_full[:, 8 * j : 8 * j + 8, :] = pltpu.roll(
            gathered.reshape(MP * 8, 4 * RANK2), (4 - j) % 4 * RANK2, axis=1
        ).reshape(MP, 8, 4 * RANK2)
    terms = lax.dot_general(
        msg[...].reshape(S, 2 * HS), lr_full[...].reshape(S, 4 * RANK2).astype(BF16), TN,
        preferred_element_type=F32,
    )
    lane = lax.broadcasted_iota(jnp.int32, (HS, 4 * RANK2), 1)
    adapter_send[...] = jnp.where(lane < RANK2 // 2, terms[:HS], terms[HS:]).reshape(8, 8, 4 * RANK2)

    for k in range(8):
        dst_mp = 8 * gb + k
        me = jnp.logical_and(p == ga, dst_mp == m)

        @pl.when(jnp.logical_not(me))
        def _():
            pltpu.make_async_remote_copy(
                src_ref=adapter_send.at[k], dst_ref=adapter_recv.at[p], send_sem=ad_send, recv_sem=ad_recv,
                device_id=(ga, dst_mp), device_id_type=MESH,
            ).start()

        @pl.when(me)
        def _():
            pltpu.make_async_copy(adapter_send.at[k], adapter_recv.at[p], own_sem.at[1]).start()

    lax.fori_loop(44, MP - 1, send, 0)

    own.wait()
    wait_bytes(lr_all, ZS - 1, lrz_send)
    wait_bytes(lr_all, ZS * (XS - 1), lrx_send)

    @pl.when(self_adapter)
    def _():
        wait_bytes(adapter_send, 1, own_sem.at[1])
        wait_bytes(adapter_send, 7, ad_send)
        wait_bytes(adapter_recv, 7, ad_recv)

    @pl.when(jnp.logical_not(self_adapter))
    def _():
        wait_bytes(adapter_send, 8, ad_send)
        wait_bytes(adapter_recv, 8, ad_recv)

    wait_bytes(msg, MP - 1, send_sem)
    wait_bytes(recv, MP - 1, recv_sem)


def owner_kernel(recv, up, adapter_recv, qg_in, key_out, value_out, lrg_out, aug_out, qg_out):
    for j in range(MP // 2):
        a = recv[2 * j]
        b = recv[2 * j + 1]
        key_out[:, 128 * j : 128 * j + 128] = jnp.concatenate([a[:, :HS], b[:, :HS]], axis=1)
        value_out[:, 128 * j : 128 * j + 128] = jnp.concatenate([a[:, HS:], b[:, HS:]], axis=1)
    from_key = lax.dot_general(key_out[...], up[...], NT, preferred_element_type=F32)
    from_value = lax.dot_general(value_out[...], up[...], NT, preferred_element_type=F32)
    lane = lax.broadcasted_iota(jnp.int32, (OWN, RANK2), 1)
    lrg_out[...] = ADAPTER_FACTOR * jnp.where(lane < RANK2 // 2, from_key, from_value)
    aug_out[...] = ADAPTER_FACTOR * jnp.sum(adapter_recv[...], axis=0)[:, :RANK2]
    qg_out[...] = qg_in[...]


def local(query, kv_cache, out_grad, source_lengths, target_lengths, low_rank, adapter_up_matrix):
    any_spec = pl.BlockSpec(memory_space=pl.ANY)
    smem = pl.BlockSpec(memory_space=pltpu.SMEM)
    vmem = pl.BlockSpec(memory_space=pltpu.VMEM)
    recv, adapter_recv, qg = pl.pallas_call(
        exchange_kernel,
        out_shape=(
            jax.ShapeDtypeStruct((MP, OWN, 2 * HS), BF16),
            jax.ShapeDtypeStruct((DP, 8, 4 * RANK2), F32),
            jax.ShapeDtypeStruct((TQ, HS), BF16),
        ),
        in_specs=[any_spec, any_spec, any_spec, smem, smem, any_spec],
        out_specs=(any_spec, any_spec, vmem),
        scratch_shapes=[
            pltpu.VMEM((TQ, HS), BF16),
            pltpu.VMEM((S, 2 * HS), BF16),
            pltpu.VMEM((TQ, HS), BF16),
            pltpu.VMEM((OWN, RANK2), BF16),
            pltpu.VMEM((2 * TQ, 2 * HS), BF16),
            pltpu.VMEM((S, TQ), F32),
            pltpu.VMEM((S, TQ), F32),
            pltpu.VMEM((S, TQ), BF16),
            pltpu.VMEM((MP, OWN, 2 * HS), BF16),
            pltpu.VMEM((MP, 8, 4 * RANK2), BF16),
            pltpu.VMEM((MP, OWN, 4 * RANK2), F32),
            pltpu.VMEM((8, 8, 4 * RANK2), F32),
            pltpu.SemaphoreType.DMA((4,)),
            pltpu.SemaphoreType.DMA,
            pltpu.SemaphoreType.DMA,
            pltpu.SemaphoreType.DMA,
            pltpu.SemaphoreType.DMA,
            pltpu.SemaphoreType.DMA,
            pltpu.SemaphoreType.DMA,
            pltpu.SemaphoreType.DMA,
            pltpu.SemaphoreType.DMA,
            pltpu.SemaphoreType.DMA((2,)),
        ],
        compiler_params=pltpu.CompilerParams(
            collective_id=0, has_side_effects=True, vmem_limit_bytes=40 << 20
        ),
        name="exchange",
    )(query, kv_cache, out_grad, source_lengths, target_lengths, low_rank)
    key_gradient, value_grad, low_rank_gradient, adapter_up_gradient, query_grad = pl.pallas_call(
        owner_kernel,
        out_shape=(
            jax.ShapeDtypeStruct((OWN, MP * HS), BF16),
            jax.ShapeDtypeStruct((OWN, MP * HS), BF16),
            jax.ShapeDtypeStruct((OWN, RANK2), F32),
            jax.ShapeDtypeStruct((8, RANK2), F32),
            jax.ShapeDtypeStruct((TQ, HS), BF16),
        ),
        in_specs=[vmem] * 4,
        out_specs=(vmem,) * 5,
        name="owner",
    )(recv, adapter_up_matrix, adapter_recv, qg)
    return query_grad, key_gradient, value_grad, low_rank_gradient, adapter_up_gradient


def solution(mesh):
    in_specs = (
        P("dp", "mp"),
        P("dp", "mp"),
        P("dp", "mp"),
        P("dp", None),
        P("dp", None),
        P(("dp", "mp"), None),
        P(),
    )
    out_specs = (
        P("dp", "mp"),
        P(("dp", "mp"), None),
        P(("dp", "mp"), None),
        P(("dp", "mp"), None),
        P(("dp", "mp"), None),
    )
    return jax.shard_map(local, mesh=mesh, in_specs=in_specs, out_specs=out_specs, check_vma=False)
```

```python
import functools

import jax
import jax.numpy as jnp
from jax import lax
from jax.experimental import pallas as pl
from jax.experimental.pallas import tpu as pltpu
from jax.sharding import PartitionSpec as P

HS = 64
XS, ZS = 4, 16
MP = XS * ZS
DP = 8
NDOC = 8
TQ = 256
S = 2048
OWN = S // MP
RANK2 = 32
ROWS = 256
ADAPTER_FACTOR = 2.0
VMEM_LIMIT = 63 << 20
MESH = pl.DeviceIdType.MESH
F32 = jnp.float32
BF16 = jnp.bfloat16
NT = (((1,), (1,)), ((), ()))
TN = (((0,), (0,)), ((), ()))


def fold8(x):
    return jnp.sum(x.reshape(x.shape[0] // 8, 8, x.shape[1]), axis=0)


def far_first(u):
    half = (u + 1) // 2
    return jnp.where(u % 2 == 1, 8 - half, 8 + half) % ZS


def exchange_kernel(
    q_hbm, kv_hbm, g_hbm, slen, tlen, lr_hbm,
    recv, adapter_recv, qg_out,
    kv_v, lr_v, w1, expo_s, dprob_s, ds_s, msg, lr_all, lr_full, adapter_send,
    in_sem, send_sem, recv_sem, lrz_send, lrz_recv, lrx_send, lrx_recv, ad_send, ad_recv, own_sem,
):
    p = lax.axis_index("dp")
    m = lax.axis_index("mp")
    x = m // ZS
    z = m % ZS
    ga = m // 8
    gb = m % 8
    self_adapter = jnp.logical_and(p == ga, gb == ga)

    barrier = pltpu.get_barrier_semaphore()

    def greet(s, _):
        pl.semaphore_signal(barrier, inc=1, device_id=(p, (m + s) % MP), device_id_type=MESH)
        return 0

    lax.fori_loop(1, MP, greet, 0)
    src_head = 8 * p + m // 8
    for j in range(DP):
        not_me = jnp.logical_not(jnp.logical_and(p == j, src_head == m))

        @pl.when(not_me)
        def _():
            pl.semaphore_signal(barrier, inc=1, device_id=(j, src_head), device_id_type=MESH)

    loads = [
        pltpu.make_async_copy(a, b, in_sem.at[i])
        for i, (a, b) in enumerate(
            (
                (q_hbm, w1.at[0:HS, 0:TQ]),
                (g_hbm, w1.at[HS : 2 * HS, TQ : 2 * TQ]),
                (kv_hbm, kv_v),
                (lr_hbm, lr_v),
            )
        )
    ]
    for c in loads:
        c.start()

    col = lax.broadcasted_iota(jnp.int32, (8, TQ), 1)
    lo = jnp.zeros((8, TQ), jnp.int32)
    hi = jnp.zeros((8, TQ), jnp.int32)
    start = jnp.int32(0)
    for k in range(NDOC):
        width = slen[0, k]
        hi = hi + jnp.where(col >= start, width, 0)
        start = start + tlen[0, k]
        lo = lo + jnp.where(col >= start, width, 0)
    lo = lo[0:1]
    hi = hi[0:1]

    zero = jnp.zeros((HS, TQ), BF16)
    w1[0:HS, TQ : 2 * TQ] = zero
    w1[HS : 2 * HS, 0:TQ] = zero
    loads[0].wait()
    loads[1].wait()
    loads[2].wait()

    row = lax.broadcasted_iota(jnp.int32, (ROWS, TQ), 0)

    def first(i, carry):
        total, weighted = carry
        base = pl.multiple_of(i * ROWS, ROWS)
        both = jnp.dot(kv_v[pl.ds(base, ROWS), :], w1[...], preferred_element_type=F32)
        dprob = both[:, TQ:]
        pos = row + base
        allowed = jnp.logical_and(pos >= lo, pos < hi)
        expo = jnp.where(allowed, jnp.exp(both[:, :TQ]), 0.0)
        expo_s[pl.ds(base, ROWS), :] = expo
        dprob_s[pl.ds(base, ROWS), :] = dprob
        return total + fold8(expo), weighted + fold8(expo * dprob)

    zeros = jnp.zeros((8, TQ), F32)
    total, weighted = lax.fori_loop(0, S // ROWS, first, (zeros, zeros))
    total = jnp.sum(total, axis=0, keepdims=True)
    delta = jnp.sum(weighted, axis=0, keepdims=True) / total
    scale = 1.0 / total

    def second(i, _):
        base = pl.multiple_of(i * ROWS, ROWS)
        prob = expo_s[pl.ds(base, ROWS), :] * scale
        ds = (prob * (dprob_s[pl.ds(base, ROWS), :] - delta)).astype(BF16)
        ds_s[pl.ds(base, ROWS), :] = ds
        both = jnp.concatenate([ds, prob.astype(BF16)], axis=1)
        grads = lax.dot_general(both, w1[...], NT, preferred_element_type=F32).astype(BF16)
        msg[pl.ds(pl.multiple_of(i * (ROWS // OWN), ROWS // OWN), ROWS // OWN)] = grads.reshape(
            ROWS // OWN, OWN, 2 * HS
        )
        return 0

    lax.fori_loop(0, S // ROWS, second, 0)

    loads[3].wait()
    lr = lr_v[...].astype(F32)
    packed = jnp.concatenate([lr[8 * j : 8 * j + 8] for j in range(4)], axis=1).astype(BF16)
    lr_all[pl.ds(m, 1)] = packed.reshape(1, 8, 4 * RANK2)

    pl.semaphore_wait(barrier, MP - 1 + DP - self_adapter.astype(jnp.int32))

    def lr_z(s, _):
        peer = x * ZS + (z + s) % ZS
        pltpu.make_async_remote_copy(
            src_ref=lr_all.at[m], dst_ref=lr_all.at[m], send_sem=lrz_send, recv_sem=lrz_recv,
            device_id=(p, peer), device_id_type=MESH,
        ).start()
        return 0

    lax.fori_loop(1, ZS, lr_z, 0)

    def send(s, _):
        peer = ((x + (s + 1) % XS) % XS) * ZS + (z + far_first(s // XS)) % ZS
        pltpu.make_async_remote_copy(
            src_ref=msg.at[peer], dst_ref=recv.at[m], send_sem=send_sem, recv_sem=recv_sem,
            device_id=(p, peer), device_id_type=MESH,
        ).start()
        return 0

    own = pltpu.make_async_copy(msg.at[m], recv.at[m], own_sem.at[0])
    own.start()
    lax.fori_loop(0, 24, send, 0)

    qg_out[...] = lax.dot_general(kv_v[...], ds_s[...], TN, preferred_element_type=F32)[:HS].astype(BF16)

    def wait_bytes(ref, count, sem):
        pltpu.make_async_copy(ref.at[pl.ds(0, count)], ref.at[pl.ds(0, count)], sem).wait()

    wait_bytes(lr_all, ZS - 1, lrz_recv)
    mine = lr_all.at[pl.ds(pl.multiple_of(x * ZS, ZS), ZS)]
    for j in range(1, XS):
        pltpu.make_async_remote_copy(
            src_ref=mine, dst_ref=mine, send_sem=lrx_send, recv_sem=lrx_recv,
            device_id=(p, ((x + j) % XS) * ZS + z), device_id_type=MESH,
        ).start()

    lax.fori_loop(24, 44, send, 0)

    wait_bytes(lr_all, ZS * (XS - 1), lrx_recv)
    gathered = lr_all[...].astype(F32)
    for j in range(4):
        lr_full[:, 8 * j : 8 * j + 8, :] = pltpu.roll(
            gathered.reshape(MP * 8, 4 * RANK2), (4 - j) % 4 * RANK2, axis=1
        ).reshape(MP, 8, 4 * RANK2)
    terms = lax.dot_general(
        msg[...].reshape(S, 2 * HS), lr_full[...].reshape(S, 4 * RANK2).astype(BF16), TN,
        preferred_element_type=F32,
    )
    lane = lax.broadcasted_iota(jnp.int32, (HS, 4 * RANK2), 1)
    adapter_send[...] = jnp.where(lane < RANK2 // 2, terms[:HS], terms[HS:]).reshape(8, 8, 4 * RANK2)

    for k in range(8):
        dst_mp = 8 * gb + k
        me = jnp.logical_and(p == ga, dst_mp == m)

        @pl.when(jnp.logical_not(me))
        def _():
            pltpu.make_async_remote_copy(
                src_ref=adapter_send.at[k], dst_ref=adapter_recv.at[p], send_sem=ad_send, recv_sem=ad_recv,
                device_id=(ga, dst_mp), device_id_type=MESH,
            ).start()

        @pl.when(me)
        def _():
            pltpu.make_async_copy(adapter_send.at[k], adapter_recv.at[p], own_sem.at[1]).start()

    lax.fori_loop(44, MP - 1, send, 0)

    own.wait()
    wait_bytes(lr_all, ZS - 1, lrz_send)
    wait_bytes(lr_all, ZS * (XS - 1), lrx_send)

    @pl.when(self_adapter)
    def _():
        wait_bytes(adapter_send, 1, own_sem.at[1])
        wait_bytes(adapter_send, 7, ad_send)
        wait_bytes(adapter_recv, 7, ad_recv)

    @pl.when(jnp.logical_not(self_adapter))
    def _():
        wait_bytes(adapter_send, 8, ad_send)
        wait_bytes(adapter_recv, 8, ad_recv)

    wait_bytes(msg, MP - 1, send_sem)
    wait_bytes(recv, MP - 1, recv_sem)


def owner_kernel(recv, up, adapter_recv, qg_in, key_out, value_out, lrg_out, aug_out, qg_out):
    for j in range(MP // 2):
        a = recv[2 * j]
        b = recv[2 * j + 1]
        key_out[:, 128 * j : 128 * j + 128] = jnp.concatenate([a[:, :HS], b[:, :HS]], axis=1)
        value_out[:, 128 * j : 128 * j + 128] = jnp.concatenate([a[:, HS:], b[:, HS:]], axis=1)
    from_key = lax.dot_general(key_out[...], up[...], NT, preferred_element_type=F32)
    from_value = lax.dot_general(value_out[...], up[...], NT, preferred_element_type=F32)
    lane = lax.broadcasted_iota(jnp.int32, (OWN, RANK2), 1)
    lrg_out[...] = ADAPTER_FACTOR * jnp.where(lane < RANK2 // 2, from_key, from_value)
    aug_out[...] = ADAPTER_FACTOR * jnp.sum(adapter_recv[...], axis=0)[:, :RANK2]
    qg_out[...] = qg_in[...]


def local(query, kv_cache, out_grad, source_lengths, target_lengths, low_rank, adapter_up_matrix):
    any_spec = pl.BlockSpec(memory_space=pl.ANY)
    smem = pl.BlockSpec(memory_space=pltpu.SMEM)
    vmem = pl.BlockSpec(memory_space=pltpu.VMEM)
    recv, adapter_recv, qg = pl.pallas_call(
        exchange_kernel,
        out_shape=(
            jax.ShapeDtypeStruct((MP, OWN, 2 * HS), BF16),
            jax.ShapeDtypeStruct((DP, 8, 4 * RANK2), F32),
            jax.ShapeDtypeStruct((HS, TQ), BF16),
        ),
        in_specs=[any_spec, any_spec, any_spec, smem, smem, any_spec],
        out_specs=(any_spec, any_spec, vmem),
        scratch_shapes=[
            pltpu.VMEM((S, 2 * HS), BF16),
            pltpu.VMEM((OWN, RANK2), BF16),
            pltpu.VMEM((2 * HS, 2 * TQ), BF16),
            pltpu.VMEM((S, TQ), F32),
            pltpu.VMEM((S, TQ), F32),
            pltpu.VMEM((S, TQ), BF16),
            pltpu.VMEM((MP, OWN, 2 * HS), BF16),
            pltpu.VMEM((MP, 8, 4 * RANK2), BF16),
            pltpu.VMEM((MP, OWN, 4 * RANK2), F32),
            pltpu.VMEM((8, 8, 4 * RANK2), F32),
            pltpu.SemaphoreType.DMA((4,)),
            pltpu.SemaphoreType.DMA,
            pltpu.SemaphoreType.DMA,
            pltpu.SemaphoreType.DMA,
            pltpu.SemaphoreType.DMA,
            pltpu.SemaphoreType.DMA,
            pltpu.SemaphoreType.DMA,
            pltpu.SemaphoreType.DMA,
            pltpu.SemaphoreType.DMA,
            pltpu.SemaphoreType.DMA((2,)),
        ],
        compiler_params=pltpu.CompilerParams(
            collective_id=0, has_side_effects=True, vmem_limit_bytes=VMEM_LIMIT
        ),
        name="exchange",
    )(query.T, kv_cache, out_grad.T, source_lengths, target_lengths, low_rank)
    key_gradient, value_grad, low_rank_gradient, adapter_up_gradient, query_grad = pl.pallas_call(
        owner_kernel,
        out_shape=(
            jax.ShapeDtypeStruct((OWN, MP * HS), BF16),
            jax.ShapeDtypeStruct((OWN, MP * HS), BF16),
            jax.ShapeDtypeStruct((OWN, RANK2), F32),
            jax.ShapeDtypeStruct((8, RANK2), F32),
            jax.ShapeDtypeStruct((HS, TQ), BF16),
        ),
        in_specs=[vmem] * 4,
        out_specs=(vmem,) * 5,
        compiler_params=pltpu.CompilerParams(vmem_limit_bytes=VMEM_LIMIT),
        name="owner",
    )(recv, adapter_up_matrix, adapter_recv, qg)
    return query_grad.T, key_gradient, value_grad, low_rank_gradient, adapter_up_gradient


def solution(mesh):
    in_specs = (
        P("dp", "mp"),
        P("dp", "mp"),
        P("dp", "mp"),
        P("dp", None),
        P("dp", None),
        P(("dp", "mp"), None),
        P(),
    )
    out_specs = (
        P("dp", "mp"),
        P(("dp", "mp"), None),
        P(("dp", "mp"), None),
        P(("dp", "mp"), None),
        P(("dp", "mp"), None),
    )
    return jax.shard_map(local, mesh=mesh, in_specs=in_specs, out_specs=out_specs, check_vma=False)
```

```python
import functools

import jax
import jax.numpy as jnp
from jax import lax
from jax.experimental import pallas as pl
from jax.experimental.pallas import tpu as pltpu
from jax.sharding import PartitionSpec as P

HS = 64
XS, ZS = 4, 16
MP = XS * ZS
DP = 8
NDOC = 8
TQ = 256
S = 2048
OWN = S // MP
RANK2 = 32
ROWS = 256
ADAPTER_FACTOR = 2.0
VMEM_LIMIT = 63 << 20
MESH = pl.DeviceIdType.MESH
F32 = jnp.float32
BF16 = jnp.bfloat16
NT = (((1,), (1,)), ((), ()))
TN = (((0,), (0,)), ((), ()))


def fold8(x):
    return jnp.sum(x.reshape(x.shape[0] // 8, 8, x.shape[1]), axis=0)


Z_ORDER = (8, 1, 15, 7, 9, 2, 14, 6, 10, 3, 13, 5, 11, 4, 12, 0)
ORDER = [(dx, dz) for dx in (2, 1, 3, 0) for dz in Z_ORDER if (dx, dz) != (0, 0)]


def exchange_kernel(
    q_hbm, kv_hbm, g_hbm, slen, tlen, lr_hbm,
    recv, adapter_recv, qg_out,
    kv_v, lr_v, w1, expo_s, dprob_s, ds_s, msg, lr_all, lr_full, term_s, adapter_send,
    in_sem, send_sem, recv_sem, lrz_send, lrz_recv, lrx_send, lrx_recv, ad_send, ad_recv, own_sem,
):
    p = lax.axis_index("dp")
    m = lax.axis_index("mp")
    x = lax.div(m, ZS)
    z = lax.rem(m, ZS)
    ga = lax.div(m, 8)
    gb = lax.rem(m, 8)
    self_adapter = jnp.logical_and(p == ga, gb == ga)

    barrier = pltpu.get_barrier_semaphore()

    def peer_of(dx, dz):
        return lax.rem(x + dx, XS) * ZS + lax.rem(z + dz, ZS)

    for dx, dz in ORDER:
        pl.semaphore_signal(barrier, inc=1, device_id=(p, peer_of(dx, dz)), device_id_type=MESH)
    src_head = 8 * p + ga
    for j in range(DP):
        not_me = jnp.logical_not(jnp.logical_and(p == j, src_head == m))

        @pl.when(not_me)
        def _():
            pl.semaphore_signal(barrier, inc=1, device_id=(j, src_head), device_id_type=MESH)

    loads = [
        pltpu.make_async_copy(a, b, in_sem.at[i])
        for i, (a, b) in enumerate(
            (
                (q_hbm, w1.at[0:HS, 0:TQ]),
                (g_hbm, w1.at[HS : 2 * HS, TQ : 2 * TQ]),
                (kv_hbm, kv_v),
                (lr_hbm, lr_v),
            )
        )
    ]
    for c in loads:
        c.start()

    col = lax.broadcasted_iota(jnp.int32, (8, TQ), 1)
    lo = jnp.zeros((8, TQ), jnp.int32)
    hi = jnp.zeros((8, TQ), jnp.int32)
    start = jnp.int32(0)
    for k in range(NDOC):
        width = slen[0, k]
        hi = hi + jnp.where(col >= start, width, 0)
        start = start + tlen[0, k]
        lo = lo + jnp.where(col >= start, width, 0)
    lo = lo[0:1]
    hi = hi[0:1]

    zero = jnp.zeros((HS, TQ), BF16)
    w1[0:HS, TQ : 2 * TQ] = zero
    w1[HS : 2 * HS, 0:TQ] = zero
    loads[0].wait()
    loads[1].wait()
    loads[2].wait()

    row = lax.broadcasted_iota(jnp.int32, (ROWS, TQ), 0)

    def first(i, carry):
        total, weighted = carry
        base = pl.multiple_of(i * ROWS, ROWS)
        both = jnp.dot(kv_v[pl.ds(base, ROWS), :], w1[...], preferred_element_type=F32)
        dprob = both[:, TQ:]
        pos = row + base
        allowed = jnp.logical_and(pos >= lo, pos < hi)
        expo = jnp.where(allowed, jnp.exp(both[:, :TQ]), 0.0)
        expo_s[pl.ds(base, ROWS), :] = expo
        dprob_s[pl.ds(base, ROWS), :] = dprob
        return total + fold8(expo), weighted + fold8(expo * dprob)

    zeros = jnp.zeros((8, TQ), F32)
    total, weighted = lax.fori_loop(0, S // ROWS, first, (zeros, zeros))
    total = jnp.sum(total, axis=0, keepdims=True)
    delta = jnp.sum(weighted, axis=0, keepdims=True) / total
    scale = 1.0 / total

    def second(i, _):
        base = pl.multiple_of(i * ROWS, ROWS)
        prob = expo_s[pl.ds(base, ROWS), :] * scale
        ds = (prob * (dprob_s[pl.ds(base, ROWS), :] - delta)).astype(BF16)
        ds_s[pl.ds(base, ROWS), :] = ds
        both = jnp.concatenate([ds, prob.astype(BF16)], axis=1)
        grads = lax.dot_general(both, w1[...], NT, preferred_element_type=F32).astype(BF16)
        msg[pl.ds(pl.multiple_of(i * (ROWS // OWN), ROWS // OWN), ROWS // OWN)] = grads.reshape(
            ROWS // OWN, OWN, 2 * HS
        )
        return 0

    lax.fori_loop(0, S // ROWS, second, 0)

    loads[3].wait()
    lr = lr_v[...].astype(F32)
    packed = jnp.concatenate([lr[8 * j : 8 * j + 8] for j in range(4)], axis=1).astype(BF16)
    lr_all[pl.ds(m, 1)] = packed.reshape(1, 8, 4 * RANK2)

    pl.semaphore_wait(barrier, MP - 1 + DP - self_adapter.astype(jnp.int32))

    for dz in Z_ORDER[:-1]:
        pltpu.make_async_remote_copy(
            src_ref=lr_all.at[m], dst_ref=lr_all.at[m], send_sem=lrz_send, recv_sem=lrz_recv,
            device_id=(p, peer_of(0, dz)), device_id_type=MESH,
        ).start()

    def send(first_one, last_one):
        for dx, dz in ORDER[first_one:last_one]:
            peer = peer_of(dx, dz)
            pltpu.make_async_remote_copy(
                src_ref=msg.at[peer], dst_ref=recv.at[m], send_sem=send_sem, recv_sem=recv_sem,
                device_id=(p, peer), device_id_type=MESH,
            ).start()

    own = pltpu.make_async_copy(msg.at[m], recv.at[m], own_sem.at[0])
    own.start()
    send(0, 24)

    qg_out[...] = lax.dot_general(kv_v[...], ds_s[...], TN, preferred_element_type=F32)[:HS].astype(BF16)

    def wait_bytes(ref, count, sem):
        pltpu.make_async_copy(ref.at[pl.ds(0, count)], ref.at[pl.ds(0, count)], sem).wait()

    wait_bytes(lr_all, ZS - 1, lrz_recv)
    mine = lr_all.at[pl.ds(pl.multiple_of(x * ZS, ZS), ZS)]
    for j in (2, 1, 3):
        pltpu.make_async_remote_copy(
            src_ref=mine, dst_ref=mine, send_sem=lrx_send, recv_sem=lrx_recv,
            device_id=(p, peer_of(j, 0)), device_id_type=MESH,
        ).start()

    send(24, 40)

    wait_bytes(lr_all, ZS * (XS - 1), lrx_recv)
    gathered = lr_all[...].astype(F32)
    for j in range(4):
        lr_full[:, 8 * j : 8 * j + 8, :] = pltpu.roll(
            gathered.reshape(MP * 8, 4 * RANK2), (4 - j) % 4 * RANK2, axis=1
        ).reshape(MP, 8, 4 * RANK2)
    terms = lax.dot_general(
        msg[...].reshape(S, 2 * HS), lr_full[...].reshape(S, 4 * RANK2).astype(BF16), TN,
        preferred_element_type=F32,
    )
    lane = lax.broadcasted_iota(jnp.int32, (HS, 4 * RANK2), 1)
    term_s[...] = jnp.where(lane < RANK2 // 2, terms[:HS], terms[HS:])
    group = lax.broadcasted_iota(jnp.int32, (HS // 4, 4 * RANK2), 1) // RANK2
    full = term_s[pl.ds(0, HS // 4, stride=4), :]
    for j in range(1, 4):
        full = jnp.where(
            group == j, pltpu.roll(term_s[pl.ds(j, HS // 4, stride=4), :], j * RANK2, axis=1), full
        )
    for k in range(8):
        adapter_send[k] = full[2 * k : 2 * k + 2]

    for k in range(8):
        dst_mp = 8 * gb + k
        me = jnp.logical_and(p == ga, dst_mp == m)

        @pl.when(jnp.logical_not(me))
        def _():
            pltpu.make_async_remote_copy(
                src_ref=adapter_send.at[k], dst_ref=adapter_recv.at[p], send_sem=ad_send, recv_sem=ad_recv,
                device_id=(ga, dst_mp), device_id_type=MESH,
            ).start()

        @pl.when(me)
        def _():
            pltpu.make_async_copy(adapter_send.at[k], adapter_recv.at[p], own_sem.at[1]).start()

    send(40, MP - 1)

    own.wait()
    wait_bytes(lr_all, ZS - 1, lrz_send)
    wait_bytes(lr_all, ZS * (XS - 1), lrx_send)

    @pl.when(self_adapter)
    def _():
        wait_bytes(adapter_send, 1, own_sem.at[1])
        wait_bytes(adapter_send, 7, ad_send)
        wait_bytes(adapter_recv, 7, ad_recv)

    @pl.when(jnp.logical_not(self_adapter))
    def _():
        wait_bytes(adapter_send, 8, ad_send)
        wait_bytes(adapter_recv, 8, ad_recv)

    wait_bytes(msg, MP - 1, send_sem)
    wait_bytes(recv, MP - 1, recv_sem)


def owner_kernel(
    recv, up_hbm, adapter_recv, qg_in, key_out, value_out, lrg_out, aug_out, qg_out,
    recv_v, grads, up, terms, qg_v, in_sem, out_sem, side_sem,
):
    parts = 4
    heads = MP // parts
    width = heads * HS
    arrive = [
        pltpu.make_async_copy(
            recv.at[pl.ds(c * heads, heads)], recv_v.at[pl.ds(c * heads, heads)], in_sem.at[c]
        )
        for c in range(parts)
    ]
    side = [
        pltpu.make_async_copy(a, b, side_sem.at[i])
        for i, (a, b) in enumerate(((up_hbm, up), (adapter_recv, terms), (qg_in, qg_v)))
    ]
    for copy in arrive + side:
        copy.start()
    leave = []
    for c in range(parts):
        arrive[c].wait()
        for j in range(c * heads // 2, (c + 1) * heads // 2):
            a = recv_v[2 * j]
            b = recv_v[2 * j + 1]
            cols = slice(128 * j, 128 * j + 128)
            grads[0:OWN, cols] = jnp.concatenate([a[:, :HS], b[:, :HS]], axis=1)
            grads[OWN : 2 * OWN, cols] = jnp.concatenate([a[:, HS:], b[:, HS:]], axis=1)
        cols = pl.ds(c * width, width)
        for i, out in enumerate((key_out, value_out)):
            copy = pltpu.make_async_copy(
                grads.at[pl.ds(i * OWN, OWN), cols], out.at[:, cols], out_sem.at[2 * c + i]
            )
            copy.start()
            leave.append(copy)
    for copy in side:
        copy.wait()
    back = pltpu.make_async_copy(qg_v, qg_out, side_sem.at[3])
    back.start()
    total = ADAPTER_FACTOR * jnp.sum(terms[...], axis=0)
    for r in range(8):
        aug_out[r : r + 1, :] = total[r // 4 : r // 4 + 1, r % 4 * RANK2 : (r % 4 + 1) * RANK2]
    both = lax.dot_general(grads[...], up[...], NT, preferred_element_type=F32)
    lane = lax.broadcasted_iota(jnp.int32, (OWN, RANK2), 1)
    lrg_out[...] = ADAPTER_FACTOR * jnp.where(lane < RANK2 // 2, both[:OWN], both[OWN:])
    for copy in leave:
        copy.wait()
    back.wait()


def local(query, kv_cache, out_grad, source_lengths, target_lengths, low_rank, adapter_up_matrix):
    any_spec = pl.BlockSpec(memory_space=pl.ANY)
    smem = pl.BlockSpec(memory_space=pltpu.SMEM)
    vmem = pl.BlockSpec(memory_space=pltpu.VMEM)
    recv, adapter_recv, qg = pl.pallas_call(
        exchange_kernel,
        out_shape=(
            jax.ShapeDtypeStruct((MP, OWN, 2 * HS), BF16),
            jax.ShapeDtypeStruct((DP, 2, 4 * RANK2), F32),
            jax.ShapeDtypeStruct((HS, TQ), BF16),
        ),
        in_specs=[any_spec, any_spec, any_spec, smem, smem, any_spec],
        out_specs=(any_spec, any_spec, vmem),
        scratch_shapes=[
            pltpu.VMEM((S, 2 * HS), BF16),
            pltpu.VMEM((OWN, RANK2), BF16),
            pltpu.VMEM((2 * HS, 2 * TQ), BF16),
            pltpu.VMEM((S, TQ), F32),
            pltpu.VMEM((S, TQ), F32),
            pltpu.VMEM((S, TQ), BF16),
            pltpu.VMEM((MP, OWN, 2 * HS), BF16),
            pltpu.VMEM((MP, 8, 4 * RANK2), BF16),
            pltpu.VMEM((MP, OWN, 4 * RANK2), F32),
            pltpu.VMEM((HS, 4 * RANK2), F32),
            pltpu.VMEM((8, 2, 4 * RANK2), F32),
            pltpu.SemaphoreType.DMA((4,)),
            pltpu.SemaphoreType.DMA,
            pltpu.SemaphoreType.DMA,
            pltpu.SemaphoreType.DMA,
            pltpu.SemaphoreType.DMA,
            pltpu.SemaphoreType.DMA,
            pltpu.SemaphoreType.DMA,
            pltpu.SemaphoreType.DMA,
            pltpu.SemaphoreType.DMA,
            pltpu.SemaphoreType.DMA((2,)),
        ],
        compiler_params=pltpu.CompilerParams(
            collective_id=0, has_side_effects=True, vmem_limit_bytes=VMEM_LIMIT
        ),
        name="exchange",
    )(query.T, kv_cache, out_grad.T, source_lengths, target_lengths, low_rank)
    key_gradient, value_grad, low_rank_gradient, adapter_up_gradient, query_grad = pl.pallas_call(
        owner_kernel,
        out_shape=(
            jax.ShapeDtypeStruct((OWN, MP * HS), BF16),
            jax.ShapeDtypeStruct((OWN, MP * HS), BF16),
            jax.ShapeDtypeStruct((OWN, RANK2), F32),
            jax.ShapeDtypeStruct((8, RANK2), F32),
            jax.ShapeDtypeStruct((HS, TQ), BF16),
        ),
        in_specs=[any_spec] * 4,
        out_specs=(any_spec, any_spec, vmem, vmem, any_spec),
        scratch_shapes=[
            pltpu.VMEM((MP, OWN, 2 * HS), BF16),
            pltpu.VMEM((2 * OWN, MP * HS), BF16),
            pltpu.VMEM((RANK2, MP * HS), BF16),
            pltpu.VMEM((DP, 2, 4 * RANK2), F32),
            pltpu.VMEM((HS, TQ), BF16),
            pltpu.SemaphoreType.DMA((4,)),
            pltpu.SemaphoreType.DMA((8,)),
            pltpu.SemaphoreType.DMA((4,)),
        ],
        compiler_params=pltpu.CompilerParams(vmem_limit_bytes=VMEM_LIMIT),
        name="owner",
    )(recv, adapter_up_matrix, adapter_recv, qg)
    return query_grad.T, key_gradient, value_grad, low_rank_gradient, adapter_up_gradient


def solution(mesh):
    in_specs = (
        P("dp", "mp"),
        P("dp", "mp"),
        P("dp", "mp"),
        P("dp", None),
        P("dp", None),
        P(("dp", "mp"), None),
        P(),
    )
    out_specs = (
        P("dp", "mp"),
        P(("dp", "mp"), None),
        P(("dp", "mp"), None),
        P(("dp", "mp"), None),
        P(("dp", "mp"), None),
    )
    return jax.shard_map(local, mesh=mesh, in_specs=in_specs, out_specs=out_specs, check_vma=False)
```

```python
import functools

import jax
import jax.numpy as jnp
from jax import lax
from jax.experimental import pallas as pl
from jax.experimental.pallas import tpu as pltpu
from jax.sharding import PartitionSpec as P

HS = 64
XS, ZS = 4, 16
MP = XS * ZS
DP = 8
NDOC = 8
TQ = 256
S = 2048
OWN = S // MP
RANK2 = 32
ROWS = 256
ADAPTER_FACTOR = 2.0
VMEM_LIMIT = 67_043_328 - (720 << 10)
LEAVE_VMEM = 67_043_328 - (720 << 10)
MESH = pl.DeviceIdType.MESH
F32 = jnp.float32
BF16 = jnp.bfloat16
NT = (((1,), (1,)), ((), ()))
TN = (((0,), (0,)), ((), ()))


def fold8(x):
    return jnp.sum(x.reshape(x.shape[0] // 8, 8, x.shape[1]), axis=0)


Z_ORDER = (8, 1, 15, 7, 9, 2, 14, 6, 10, 3, 13, 5, 11, 4, 12, 0)
ORDER = [(dx, dz) for dx in (2, 1, 3, 0) for dz in Z_ORDER if (dx, dz) != (0, 0)]


def exchange_kernel(
    q_hbm, kv_hbm, g_hbm, slen, tlen, lr_hbm, up_hbm,
    grads, lrg_out, aug_out, qg_out,
    kv_v, lr_v, up, w1, expo_s, dprob_s, ds_s, msg, lr_all, lr_full, term_s, adapter_send, recv, adapter_recv,
    in_sem, send_sem, recv_sem, lrz_send, lrz_recv, lrx_send, lrx_recv, ad_send, ad_recv, own_sem,
):
    p = lax.axis_index("dp")
    m = lax.axis_index("mp")
    x = lax.div(m, ZS)
    z = lax.rem(m, ZS)
    ga = lax.div(m, 8)
    gb = lax.rem(m, 8)
    self_adapter = jnp.logical_and(p == ga, gb == ga)

    barrier = pltpu.get_barrier_semaphore()

    def peer_of(dx, dz):
        return lax.rem(x + dx, XS) * ZS + lax.rem(z + dz, ZS)

    for dx, dz in ORDER:
        pl.semaphore_signal(barrier, inc=1, device_id=(p, peer_of(dx, dz)), device_id_type=MESH)
    src_head = 8 * p + ga
    for j in range(DP):
        not_me = jnp.logical_not(jnp.logical_and(p == j, src_head == m))

        @pl.when(not_me)
        def _():
            pl.semaphore_signal(barrier, inc=1, device_id=(j, src_head), device_id_type=MESH)

    loads = [
        pltpu.make_async_copy(a, b, in_sem.at[i])
        for i, (a, b) in enumerate(
            (
                (q_hbm, w1.at[0:HS, 0:TQ]),
                (g_hbm, w1.at[HS : 2 * HS, TQ : 2 * TQ]),
                (kv_hbm, kv_v),
                (lr_hbm, lr_v),
                (up_hbm, up),
            )
        )
    ]
    for c in loads:
        c.start()

    col = lax.broadcasted_iota(jnp.int32, (8, TQ), 1)
    lo = jnp.zeros((8, TQ), jnp.int32)
    hi = jnp.zeros((8, TQ), jnp.int32)
    start = jnp.int32(0)
    for k in range(NDOC):
        width = slen[0, k]
        hi = hi + jnp.where(col >= start, width, 0)
        start = start + tlen[0, k]
        lo = lo + jnp.where(col >= start, width, 0)
    lo = lo[0:1]
    hi = hi[0:1]

    zero = jnp.zeros((HS, TQ), BF16)
    w1[0:HS, TQ : 2 * TQ] = zero
    w1[HS : 2 * HS, 0:TQ] = zero
    loads[0].wait()
    loads[1].wait()
    loads[2].wait()

    row = lax.broadcasted_iota(jnp.int32, (ROWS, TQ), 0)

    def first(i, carry):
        total, weighted = carry
        base = pl.multiple_of(i * ROWS, ROWS)
        both = jnp.dot(kv_v[pl.ds(base, ROWS), :], w1[...], preferred_element_type=F32)
        dprob = both[:, TQ:]
        pos = row + base
        allowed = jnp.logical_and(pos >= lo, pos < hi)
        expo = jnp.where(allowed, jnp.exp(both[:, :TQ]), 0.0)
        expo_s[pl.ds(base, ROWS), :] = expo
        dprob_s[pl.ds(base, ROWS), :] = dprob
        return total + fold8(expo), weighted + fold8(expo * dprob)

    zeros = jnp.zeros((8, TQ), F32)
    total, weighted = lax.fori_loop(0, S // ROWS, first, (zeros, zeros))
    total = jnp.sum(total, axis=0, keepdims=True)
    delta = jnp.sum(weighted, axis=0, keepdims=True) / total
    scale = 1.0 / total

    def second(i, _):
        base = pl.multiple_of(i * ROWS, ROWS)
        prob = expo_s[pl.ds(base, ROWS), :] * scale
        ds = (prob * (dprob_s[pl.ds(base, ROWS), :] - delta)).astype(BF16)
        ds_s[pl.ds(base, ROWS), :] = ds
        both = jnp.concatenate([ds, prob.astype(BF16)], axis=1)
        grads = lax.dot_general(both, w1[...], NT, preferred_element_type=F32).astype(BF16)
        msg[pl.ds(pl.multiple_of(i * (ROWS // OWN), ROWS // OWN), ROWS // OWN)] = grads.reshape(
            ROWS // OWN, OWN, 2 * HS
        )
        return 0

    lax.fori_loop(0, S // ROWS, second, 0)

    loads[3].wait()
    lr = lr_v[...].astype(F32)
    packed = jnp.concatenate([lr[8 * j : 8 * j + 8] for j in range(4)], axis=1).astype(BF16)
    lr_all[pl.ds(m, 1)] = packed.reshape(1, 8, 4 * RANK2)

    pl.semaphore_wait(barrier, MP - 1 + DP - self_adapter.astype(jnp.int32))

    for dz in Z_ORDER[:-1]:
        pltpu.make_async_remote_copy(
            src_ref=lr_all.at[m], dst_ref=lr_all.at[m], send_sem=lrz_send, recv_sem=lrz_recv,
            device_id=(p, peer_of(0, dz)), device_id_type=MESH,
        ).start()

    def send(first_one, last_one):
        for dx, dz in ORDER[first_one:last_one]:
            peer = peer_of(dx, dz)
            pltpu.make_async_remote_copy(
                src_ref=msg.at[peer], dst_ref=recv.at[m], send_sem=send_sem, recv_sem=recv_sem.at[dx],
                device_id=(p, peer), device_id_type=MESH,
            ).start()

    recv[pl.ds(m, 1)] = msg[pl.ds(m, 1)]
    send(0, 36)

    qg_out[...] = lax.dot_general(kv_v[...], ds_s[...], TN, preferred_element_type=F32)[:HS].astype(BF16)

    def wait_bytes(ref, count, sem):
        pltpu.make_async_copy(ref.at[pl.ds(0, count)], ref.at[pl.ds(0, count)], sem).wait()

    wait_bytes(lr_all, ZS - 1, lrz_recv)
    mine = lr_all.at[pl.ds(pl.multiple_of(x * ZS, ZS), ZS)]
    for j in (2, 1, 3):
        pltpu.make_async_remote_copy(
            src_ref=mine, dst_ref=mine, send_sem=lrx_send, recv_sem=lrx_recv,
            device_id=(p, peer_of(j, 0)), device_id_type=MESH,
        ).start()

    send(36, 50)

    wait_bytes(lr_all, ZS * (XS - 1), lrx_recv)
    gathered = lr_all[...].astype(F32)
    for j in range(4):
        lr_full[:, 8 * j : 8 * j + 8, :] = pltpu.roll(
            gathered.reshape(MP * 8, 4 * RANK2), (4 - j) % 4 * RANK2, axis=1
        ).reshape(MP, 8, 4 * RANK2)
    terms = lax.dot_general(
        msg[...].reshape(S, 2 * HS), lr_full[...].reshape(S, 4 * RANK2).astype(BF16), TN,
        preferred_element_type=F32,
    )
    lane = lax.broadcasted_iota(jnp.int32, (HS, 4 * RANK2), 1)
    term_s[...] = jnp.where(lane < RANK2 // 2, terms[:HS], terms[HS:])
    group = lax.broadcasted_iota(jnp.int32, (HS // 4, 4 * RANK2), 1) // RANK2
    full = term_s[pl.ds(0, HS // 4, stride=4), :]
    for j in range(1, 4):
        full = jnp.where(
            group == j, pltpu.roll(term_s[pl.ds(j, HS // 4, stride=4), :], j * RANK2, axis=1), full
        )
    for k in range(8):
        adapter_send[k] = full[2 * k : 2 * k + 2]

    for k in range(8):
        dst_mp = 8 * gb + k
        me = jnp.logical_and(p == ga, dst_mp == m)

        @pl.when(jnp.logical_not(me))
        def _():
            pltpu.make_async_remote_copy(
                src_ref=adapter_send.at[k], dst_ref=adapter_recv.at[p], send_sem=ad_send, recv_sem=ad_recv,
                device_id=(ga, dst_mp), device_id_type=MESH,
            ).start()

        @pl.when(me)
        def _():
            pltpu.make_async_copy(adapter_send.at[k], adapter_recv.at[p], own_sem).start()

    send(50, MP - 1)

    loads[4].wait()

    def place(dx):
        wait_bytes(recv, ZS if dx else ZS - 1, recv_sem.at[dx])
        column = lax.rem(x + XS - dx, XS)
        for j in range(ZS // 2):
            a = recv[column * ZS + 2 * j]
            b = recv[column * ZS + 2 * j + 1]
            lanes = pl.ds(pl.multiple_of(column * (ZS * HS) + 128 * j, 128), 128)
            grads[0:OWN, lanes] = jnp.concatenate([a[:, :HS], b[:, :HS]], axis=1)
            grads[OWN : 2 * OWN, lanes] = jnp.concatenate([a[:, HS:], b[:, HS:]], axis=1)
        lanes = pl.ds(pl.multiple_of(column * (ZS * HS), ZS * HS), ZS * HS)
        return lax.dot_general(grads[:, lanes], up[:, lanes], NT, preferred_element_type=F32)

    both = place(2)
    both = both + place(1)
    both = both + place(3)

    wait_bytes(lr_all, ZS - 1, lrz_send)
    wait_bytes(lr_all, ZS * (XS - 1), lrx_send)

    @pl.when(self_adapter)
    def _():
        wait_bytes(adapter_send, 1, own_sem)
        wait_bytes(adapter_send, 7, ad_send)
        wait_bytes(adapter_recv, 7, ad_recv)

    @pl.when(jnp.logical_not(self_adapter))
    def _():
        wait_bytes(adapter_send, 8, ad_send)
        wait_bytes(adapter_recv, 8, ad_recv)

    total = ADAPTER_FACTOR * jnp.sum(adapter_recv[...], axis=0)
    for r in range(8):
        aug_out[r : r + 1, :] = total[r // 4 : r // 4 + 1, r % 4 * RANK2 : (r % 4 + 1) * RANK2]

    wait_bytes(msg, MP - 1, send_sem)
    both = both + place(0)
    lane = lax.broadcasted_iota(jnp.int32, (OWN, RANK2), 1)
    lrg_out[...] = ADAPTER_FACTOR * jnp.where(lane < RANK2 // 2, both[:OWN], both[OWN:])


def leave_kernel(grads, lrg, aug, qg, key_out, value_out, lrg_out, aug_out, qg_out, sem):
    copies = [
        pltpu.make_async_copy(a, b, sem.at[i])
        for i, (a, b) in enumerate(
            (
                (grads.at[0:OWN], key_out),
                (grads.at[OWN : 2 * OWN], value_out),
                (lrg, lrg_out),
                (aug, aug_out),
                (qg, qg_out),
            )
        )
    ]
    for copy in copies:
        copy.start()
    for copy in copies:
        copy.wait()


def local(query, kv_cache, out_grad, source_lengths, target_lengths, low_rank, adapter_up_matrix):
    any_spec = pl.BlockSpec(memory_space=pl.ANY)
    smem = pl.BlockSpec(memory_space=pltpu.SMEM)
    vmem = pl.BlockSpec(memory_space=pltpu.VMEM)
    inside = pl.pallas_call(
        exchange_kernel,
        out_shape=(
            pltpu.VMEM((2 * OWN, MP * HS), BF16),
            pltpu.VMEM((OWN, RANK2), F32),
            pltpu.VMEM((8, RANK2), F32),
            pltpu.VMEM((HS, TQ), BF16),
        ),
        in_specs=[any_spec, any_spec, any_spec, smem, smem, any_spec, any_spec],
        out_specs=(vmem,) * 4,
        scratch_shapes=[
            pltpu.VMEM((S, 2 * HS), BF16),
            pltpu.VMEM((OWN, RANK2), BF16),
            pltpu.VMEM((RANK2, MP * HS), BF16),
            pltpu.VMEM((2 * HS, 2 * TQ), BF16),
            pltpu.VMEM((S, TQ), F32),
            pltpu.VMEM((S, TQ), F32),
            pltpu.VMEM((S, TQ), BF16),
            pltpu.VMEM((MP, OWN, 2 * HS), BF16),
            pltpu.VMEM((MP, 8, 4 * RANK2), BF16),
            pltpu.VMEM((MP, OWN, 4 * RANK2), F32),
            pltpu.VMEM((HS, 4 * RANK2), F32),
            pltpu.VMEM((8, 2, 4 * RANK2), F32),
            pltpu.VMEM((MP, OWN, 2 * HS), BF16),
            pltpu.VMEM((DP, 2, 4 * RANK2), F32),
            pltpu.SemaphoreType.DMA((5,)),
            pltpu.SemaphoreType.DMA,
            pltpu.SemaphoreType.DMA((XS,)),
            pltpu.SemaphoreType.DMA,
            pltpu.SemaphoreType.DMA,
            pltpu.SemaphoreType.DMA,
            pltpu.SemaphoreType.DMA,
            pltpu.SemaphoreType.DMA,
            pltpu.SemaphoreType.DMA,
            pltpu.SemaphoreType.DMA,
        ],
        compiler_params=pltpu.CompilerParams(
            collective_id=0, has_side_effects=True, vmem_limit_bytes=VMEM_LIMIT
        ),
        name="exchange",
    )(query.T, kv_cache, out_grad.T, source_lengths, target_lengths, low_rank, adapter_up_matrix)
    inside = [pltpu.with_memory_space_constraint(a, pltpu.VMEM) for a in inside]
    key_gradient, value_grad, low_rank_gradient, adapter_up_gradient, query_grad = pl.pallas_call(
        leave_kernel,
        out_shape=(
            jax.ShapeDtypeStruct((OWN, MP * HS), BF16),
            jax.ShapeDtypeStruct((OWN, MP * HS), BF16),
            jax.ShapeDtypeStruct((OWN, RANK2), F32),
            jax.ShapeDtypeStruct((8, RANK2), F32),
            jax.ShapeDtypeStruct((HS, TQ), BF16),
        ),
        in_specs=[vmem] * 4,
        out_specs=(any_spec,) * 5,
        scratch_shapes=[pltpu.SemaphoreType.DMA((5,))],
        compiler_params=pltpu.CompilerParams(vmem_limit_bytes=LEAVE_VMEM),
        name="leave",
    )(*inside)
    return query_grad.T, key_gradient, value_grad, low_rank_gradient, adapter_up_gradient


def solution(mesh):
    in_specs = (
        P("dp", "mp"),
        P("dp", "mp"),
        P("dp", "mp"),
        P("dp", None),
        P("dp", None),
        P(("dp", "mp"), None),
        P(),
    )
    out_specs = (
        P("dp", "mp"),
        P(("dp", "mp"), None),
        P(("dp", "mp"), None),
        P(("dp", "mp"), None),
        P(("dp", "mp"), None),
    )
    return jax.shard_map(local, mesh=mesh, in_specs=in_specs, out_specs=out_specs, check_vma=False)
```

```python
import functools

import jax
import jax.numpy as jnp
from jax import lax
from jax.experimental import pallas as pl
from jax.experimental.pallas import tpu as pltpu
from jax.sharding import PartitionSpec as P

HS = 64
XS, ZS = 4, 16
MP = XS * ZS
DP = 8
NDOC = 8
TQ = 256
S = 2048
OWN = S // MP
RANK2 = 32
ROWS = 256
ADAPTER_FACTOR = 2.0
VMEM_LIMIT = 67_043_328 - (720 << 10)
LEAVE_VMEM = 67_043_328 - (720 << 10)
MESH = pl.DeviceIdType.MESH
F32 = jnp.float32
BF16 = jnp.bfloat16
NT = (((1,), (1,)), ((), ()))
TN = (((0,), (0,)), ((), ()))


def fold8(x):
    return jnp.sum(x.reshape(x.shape[0] // 8, 8, x.shape[1]), axis=0)


Z_ORDER = (8, 1, 15, 7, 9, 2, 14, 6, 10, 3, 13, 5, 11, 4, 12, 0)
ORDER = [(dx, dz) for dx in (2, 1, 3, 0) for dz in Z_ORDER if (dx, dz) != (0, 0)]


def exchange_kernel(
    q_hbm, kv_hbm, g_hbm, slen_hbm, tlen_hbm, lr_hbm, up_hbm,
    grads, lrg_out, aug_out, qg_out,
    slen, tlen, kv_v, lr_v, up, w1, expo_s, dprob_s, ds_s, msg, lr_all, lr_full, term_s, adapter_send, recv, adapter_recv,
    in_sem, send_sem, recv_sem, lrz_send, lrz_recv, lrx_send, lrx_recv, ad_send, ad_recv, own_sem,
):
    p = lax.axis_index("dp")
    m = lax.axis_index("mp")
    x = lax.div(m, ZS)
    z = lax.rem(m, ZS)
    ga = lax.div(m, 8)
    gb = lax.rem(m, 8)
    self_adapter = jnp.logical_and(p == ga, gb == ga)

    barrier = pltpu.get_barrier_semaphore()

    def peer_of(dx, dz):
        return lax.rem(x + dx, XS) * ZS + lax.rem(z + dz, ZS)

    for dx, dz in ORDER:
        pl.semaphore_signal(barrier, inc=1, device_id=(p, peer_of(dx, dz)), device_id_type=MESH)
    src_head = 8 * p + ga
    for j in range(DP):
        not_me = jnp.logical_not(jnp.logical_and(p == j, src_head == m))

        @pl.when(not_me)
        def _():
            pl.semaphore_signal(barrier, inc=1, device_id=(j, src_head), device_id_type=MESH)

    loads = [
        pltpu.make_async_copy(a, b, in_sem.at[i])
        for i, (a, b) in enumerate(
            (
                (q_hbm, w1.at[0:HS, 0:TQ]),
                (g_hbm, w1.at[HS : 2 * HS, TQ : 2 * TQ]),
                (kv_hbm, kv_v),
                (lr_hbm, lr_v),
                (up_hbm, up),
                (slen_hbm, slen),
                (tlen_hbm, tlen),
            )
        )
    ]
    for c in loads:
        c.start()

    loads[5].wait()
    loads[6].wait()
    col = lax.broadcasted_iota(jnp.int32, (8, TQ), 1)
    lo = jnp.zeros((8, TQ), jnp.int32)
    hi = jnp.zeros((8, TQ), jnp.int32)
    start = jnp.int32(0)
    for k in range(NDOC):
        width = slen[0, k]
        hi = hi + jnp.where(col >= start, width, 0)
        start = start + tlen[0, k]
        lo = lo + jnp.where(col >= start, width, 0)
    lo = lo[0:1]
    hi = hi[0:1]

    zero = jnp.zeros((HS, TQ), BF16)
    w1[0:HS, TQ : 2 * TQ] = zero
    w1[HS : 2 * HS, 0:TQ] = zero
    loads[0].wait()
    loads[1].wait()
    loads[2].wait()

    row = lax.broadcasted_iota(jnp.int32, (ROWS, TQ), 0)

    def first(i, carry):
        total, weighted = carry
        base = pl.multiple_of(i * ROWS, ROWS)
        both = jnp.dot(kv_v[pl.ds(base, ROWS), :], w1[...], preferred_element_type=F32)
        dprob = both[:, TQ:]
        pos = row + base
        allowed = jnp.logical_and(pos >= lo, pos < hi)
        expo = jnp.where(allowed, jnp.exp(both[:, :TQ]), 0.0)
        expo_s[pl.ds(base, ROWS), :] = expo
        dprob_s[pl.ds(base, ROWS), :] = dprob
        return total + fold8(expo), weighted + fold8(expo * dprob)

    zeros = jnp.zeros((8, TQ), F32)
    total, weighted = lax.fori_loop(0, S // ROWS, first, (zeros, zeros))
    total = jnp.sum(total, axis=0, keepdims=True)
    delta = jnp.sum(weighted, axis=0, keepdims=True) / total
    scale = 1.0 / total

    def second(i, _):
        base = pl.multiple_of(i * ROWS, ROWS)
        prob = expo_s[pl.ds(base, ROWS), :] * scale
        ds = (prob * (dprob_s[pl.ds(base, ROWS), :] - delta)).astype(BF16)
        ds_s[pl.ds(base, ROWS), :] = ds
        both = jnp.concatenate([ds, prob.astype(BF16)], axis=1)
        grads = lax.dot_general(both, w1[...], NT, preferred_element_type=F32).astype(BF16)
        msg[pl.ds(pl.multiple_of(i * (ROWS // OWN), ROWS // OWN), ROWS // OWN)] = grads.reshape(
            ROWS // OWN, OWN, 2 * HS
        )
        return 0

    lax.fori_loop(0, S // ROWS, second, 0)

    loads[3].wait()
    lr = lr_v[...].astype(F32)
    packed = jnp.concatenate([lr[8 * j : 8 * j + 8] for j in range(4)], axis=1).astype(BF16)
    lr_all[pl.ds(m, 1)] = packed.reshape(1, 8, 4 * RANK2)

    pl.semaphore_wait(barrier, MP - 1 + DP - self_adapter.astype(jnp.int32))

    for dz in Z_ORDER[:-1]:
        pltpu.make_async_remote_copy(
            src_ref=lr_all.at[m], dst_ref=lr_all.at[m], send_sem=lrz_send, recv_sem=lrz_recv,
            device_id=(p, peer_of(0, dz)), device_id_type=MESH,
        ).start()

    def send(first_one, last_one):
        for dx, dz in ORDER[first_one:last_one]:
            peer = peer_of(dx, dz)
            pltpu.make_async_remote_copy(
                src_ref=msg.at[peer], dst_ref=recv.at[m], send_sem=send_sem, recv_sem=recv_sem.at[dx],
                device_id=(p, peer), device_id_type=MESH,
            ).start()

    recv[pl.ds(m, 1)] = msg[pl.ds(m, 1)]
    send(0, 36)

    qg_out[...] = lax.dot_general(kv_v[...], ds_s[...], TN, preferred_element_type=F32)[:HS].astype(BF16)

    def wait_bytes(ref, count, sem):
        pltpu.make_async_copy(ref.at[pl.ds(0, count)], ref.at[pl.ds(0, count)], sem).wait()

    wait_bytes(lr_all, ZS - 1, lrz_recv)
    mine = lr_all.at[pl.ds(pl.multiple_of(x * ZS, ZS), ZS)]
    for j in (2, 1, 3):
        pltpu.make_async_remote_copy(
            src_ref=mine, dst_ref=mine, send_sem=lrx_send, recv_sem=lrx_recv,
            device_id=(p, peer_of(j, 0)), device_id_type=MESH,
        ).start()

    send(36, 50)

    wait_bytes(lr_all, ZS * (XS - 1), lrx_recv)
    gathered = lr_all[...].astype(F32)
    for j in range(4):
        lr_full[:, 8 * j : 8 * j + 8, :] = pltpu.roll(
            gathered.reshape(MP * 8, 4 * RANK2), (4 - j) % 4 * RANK2, axis=1
        ).reshape(MP, 8, 4 * RANK2)
    terms = lax.dot_general(
        msg[...].reshape(S, 2 * HS), lr_full[...].reshape(S, 4 * RANK2).astype(BF16), TN,
        preferred_element_type=F32,
    )
    lane = lax.broadcasted_iota(jnp.int32, (HS, 4 * RANK2), 1)
    term_s[...] = jnp.where(lane < RANK2 // 2, terms[:HS], terms[HS:])
    group = lax.broadcasted_iota(jnp.int32, (HS // 4, 4 * RANK2), 1) // RANK2
    full = term_s[pl.ds(0, HS // 4, stride=4), :]
    for j in range(1, 4):
        full = jnp.where(
            group == j, pltpu.roll(term_s[pl.ds(j, HS // 4, stride=4), :], j * RANK2, axis=1), full
        )
    for k in range(8):
        adapter_send[k] = full[2 * k : 2 * k + 2]

    for k in range(8):
        dst_mp = 8 * gb + k
        me = jnp.logical_and(p == ga, dst_mp == m)

        @pl.when(jnp.logical_not(me))
        def _():
            pltpu.make_async_remote_copy(
                src_ref=adapter_send.at[k], dst_ref=adapter_recv.at[p], send_sem=ad_send, recv_sem=ad_recv,
                device_id=(ga, dst_mp), device_id_type=MESH,
            ).start()

        @pl.when(me)
        def _():
            pltpu.make_async_copy(adapter_send.at[k], adapter_recv.at[p], own_sem).start()

    send(50, MP - 1)

    loads[4].wait()

    def place(dx):
        wait_bytes(recv, ZS if dx else ZS - 1, recv_sem.at[dx])
        column = lax.rem(x + XS - dx, XS)
        for j in range(ZS // 2):
            a = recv[column * ZS + 2 * j]
            b = recv[column * ZS + 2 * j + 1]
            lanes = pl.ds(pl.multiple_of(column * (ZS * HS) + 128 * j, 128), 128)
            grads[0:OWN, lanes] = jnp.concatenate([a[:, :HS], b[:, :HS]], axis=1)
            grads[OWN : 2 * OWN, lanes] = jnp.concatenate([a[:, HS:], b[:, HS:]], axis=1)
        lanes = pl.ds(pl.multiple_of(column * (ZS * HS), ZS * HS), ZS * HS)
        return lax.dot_general(grads[:, lanes], up[:, lanes], NT, preferred_element_type=F32)

    both = place(2)
    both = both + place(1)
    both = both + place(3)

    wait_bytes(lr_all, ZS - 1, lrz_send)
    wait_bytes(lr_all, ZS * (XS - 1), lrx_send)

    @pl.when(self_adapter)
    def _():
        wait_bytes(adapter_send, 1, own_sem)
        wait_bytes(adapter_send, 7, ad_send)
        wait_bytes(adapter_recv, 7, ad_recv)

    @pl.when(jnp.logical_not(self_adapter))
    def _():
        wait_bytes(adapter_send, 8, ad_send)
        wait_bytes(adapter_recv, 8, ad_recv)

    total = ADAPTER_FACTOR * jnp.sum(adapter_recv[...], axis=0)
    for r in range(8):
        aug_out[r : r + 1, :] = total[r // 4 : r // 4 + 1, r % 4 * RANK2 : (r % 4 + 1) * RANK2]

    wait_bytes(msg, MP - 1, send_sem)
    both = both + place(0)
    lane = lax.broadcasted_iota(jnp.int32, (OWN, RANK2), 1)
    lrg_out[...] = ADAPTER_FACTOR * jnp.where(lane < RANK2 // 2, both[:OWN], both[OWN:])


def leave_kernel(grads, lrg, aug, qg, key_out, value_out, lrg_out, aug_out, qg_out, sem):
    copies = [
        pltpu.make_async_copy(a, b, sem.at[i])
        for i, (a, b) in enumerate(
            (
                (grads.at[0:OWN], key_out),
                (grads.at[OWN : 2 * OWN], value_out),
                (lrg, lrg_out),
                (aug, aug_out),
                (qg, qg_out),
            )
        )
    ]
    for copy in copies:
        copy.start()
    for copy in copies:
        copy.wait()


def local(query, kv_cache, out_grad, source_lengths, target_lengths, low_rank, adapter_up_matrix):
    any_spec = pl.BlockSpec(memory_space=pl.ANY)
    vmem = pl.BlockSpec(memory_space=pltpu.VMEM)
    inside = pl.pallas_call(
        exchange_kernel,
        out_shape=(
            pltpu.VMEM((2 * OWN, MP * HS), BF16),
            pltpu.VMEM((OWN, RANK2), F32),
            pltpu.VMEM((8, RANK2), F32),
            pltpu.VMEM((HS, TQ), BF16),
        ),
        in_specs=[any_spec] * 7,
        out_specs=(vmem,) * 4,
        scratch_shapes=[
            pltpu.SMEM((1, NDOC), jnp.int32),
            pltpu.SMEM((1, NDOC), jnp.int32),
            pltpu.VMEM((S, 2 * HS), BF16),
            pltpu.VMEM((OWN, RANK2), BF16),
            pltpu.VMEM((RANK2, MP * HS), BF16),
            pltpu.VMEM((2 * HS, 2 * TQ), BF16),
            pltpu.VMEM((S, TQ), F32),
            pltpu.VMEM((S, TQ), F32),
            pltpu.VMEM((S, TQ), BF16),
            pltpu.VMEM((MP, OWN, 2 * HS), BF16),
            pltpu.VMEM((MP, 8, 4 * RANK2), BF16),
            pltpu.VMEM((MP, OWN, 4 * RANK2), F32),
            pltpu.VMEM((HS, 4 * RANK2), F32),
            pltpu.VMEM((8, 2, 4 * RANK2), F32),
            pltpu.VMEM((MP, OWN, 2 * HS), BF16),
            pltpu.VMEM((DP, 2, 4 * RANK2), F32),
            pltpu.SemaphoreType.DMA((7,)),
            pltpu.SemaphoreType.DMA,
            pltpu.SemaphoreType.DMA((XS,)),
            pltpu.SemaphoreType.DMA,
            pltpu.SemaphoreType.DMA,
            pltpu.SemaphoreType.DMA,
            pltpu.SemaphoreType.DMA,
            pltpu.SemaphoreType.DMA,
            pltpu.SemaphoreType.DMA,
            pltpu.SemaphoreType.DMA,
        ],
        compiler_params=pltpu.CompilerParams(
            collective_id=0, has_side_effects=True, vmem_limit_bytes=VMEM_LIMIT
        ),
        name="exchange",
    )(query.T, kv_cache, out_grad.T, source_lengths, target_lengths, low_rank, adapter_up_matrix)
    inside = [pltpu.with_memory_space_constraint(a, pltpu.VMEM) for a in inside]
    key_gradient, value_grad, low_rank_gradient, adapter_up_gradient, query_grad = pl.pallas_call(
        leave_kernel,
        out_shape=(
            jax.ShapeDtypeStruct((OWN, MP * HS), BF16),
            jax.ShapeDtypeStruct((OWN, MP * HS), BF16),
            jax.ShapeDtypeStruct((OWN, RANK2), F32),
            jax.ShapeDtypeStruct((8, RANK2), F32),
            jax.ShapeDtypeStruct((HS, TQ), BF16),
        ),
        in_specs=[vmem] * 4,
        out_specs=(any_spec,) * 5,
        scratch_shapes=[pltpu.SemaphoreType.DMA((5,))],
        compiler_params=pltpu.CompilerParams(vmem_limit_bytes=LEAVE_VMEM),
        name="leave",
    )(*inside)
    return query_grad.T, key_gradient, value_grad, low_rank_gradient, adapter_up_gradient


def solution(mesh):
    in_specs = (
        P("dp", "mp"),
        P("dp", "mp"),
        P("dp", "mp"),
        P("dp", None),
        P("dp", None),
        P(("dp", "mp"), None),
        P(),
    )
    out_specs = (
        P("dp", "mp"),
        P(("dp", "mp"), None),
        P(("dp", "mp"), None),
        P(("dp", "mp"), None),
        P(("dp", "mp"), None),
    )
    return jax.shard_map(local, mesh=mesh, in_specs=in_specs, out_specs=out_specs, check_vma=False)
```

```python
import functools

import jax
import jax.numpy as jnp
from jax import lax
from jax.experimental import pallas as pl
from jax.experimental.pallas import tpu as pltpu
from jax.sharding import PartitionSpec as P

HS = 64
XS, ZS = 4, 16
MP = XS * ZS
DP = 8
NDOC = 8
TQ = 256
S = 2048
OWN = S // MP
RANK2 = 32
ROWS = 256
ADAPTER_FACTOR = 2.0
VMEM_LIMIT = 67_043_328 - (720 << 10)
LEAVE_VMEM = 67_043_328 - (720 << 10)
MESH = pl.DeviceIdType.MESH
F32 = jnp.float32
BF16 = jnp.bfloat16
NT = (((1,), (1,)), ((), ()))
TN = (((0,), (0,)), ((), ()))


def fold8(x):
    return jnp.sum(x.reshape(x.shape[0] // 8, 8, x.shape[1]), axis=0)


Z_ORDER = (8, 1, 15, 7, 9, 2, 14, 6, 10, 3, 13, 5, 11, 4, 12, 0)
ORDER = [(dx, dz) for dx in (2, 1, 3, 0) for dz in Z_ORDER if (dx, dz) != (0, 0)]


def exchange_kernel(
    q_hbm, kv_hbm, g_hbm, slen_hbm, tlen_hbm, lr_hbm, up_hbm,
    grads, lrg_out, aug_out, qg_out,
    slen, tlen, kv_v, lr_v, up, w1, expo_s, dprob_s, ds_s, msg, lr_all, lr_full, term_s, adapter_send, recv, adapter_recv,
    in_sem, send_sem, recv_sem, lrz_send, lrz_recv, lrx_send, lrx_recv, ad_send, ad_recv, own_sem,
):
    p = lax.axis_index("dp")
    m = lax.axis_index("mp")
    x = lax.div(m, ZS)
    z = lax.rem(m, ZS)
    ga = lax.div(m, 8)
    gb = lax.rem(m, 8)
    self_adapter = jnp.logical_and(p == ga, gb == ga)

    barrier = pltpu.get_barrier_semaphore()

    def peer_of(dx, dz):
        return lax.rem(x + dx, XS) * ZS + lax.rem(z + dz, ZS)

    for dx, dz in ORDER:
        pl.semaphore_signal(barrier, inc=1, device_id=(p, peer_of(dx, dz)), device_id_type=MESH)
    src_head = 8 * p + ga
    for j in range(DP):
        not_me = jnp.logical_not(jnp.logical_and(p == j, src_head == m))

        @pl.when(not_me)
        def _():
            pl.semaphore_signal(barrier, inc=1, device_id=(j, src_head), device_id_type=MESH)

    loads = [
        pltpu.make_async_copy(a, b, in_sem.at[i])
        for i, (a, b) in enumerate(
            (
                (q_hbm, w1.at[0:HS, 0:TQ]),
                (g_hbm, w1.at[HS : 2 * HS, TQ : 2 * TQ]),
                (kv_hbm, kv_v),
                (lr_hbm, lr_v),
                (up_hbm, up),
                (slen_hbm, slen),
                (tlen_hbm, tlen),
            )
        )
    ]
    for c in loads:
        c.start()

    loads[5].wait()
    loads[6].wait()
    col = lax.broadcasted_iota(jnp.int32, (8, TQ), 1)
    lo = jnp.zeros((8, TQ), jnp.int32)
    hi = jnp.zeros((8, TQ), jnp.int32)
    start = jnp.int32(0)
    for k in range(NDOC):
        width = slen[0, k]
        hi = hi + jnp.where(col >= start, width, 0)
        start = start + tlen[0, k]
        lo = lo + jnp.where(col >= start, width, 0)
    lo = lo[0:1]
    hi = hi[0:1]

    zero = jnp.zeros((HS, TQ), BF16)
    w1[0:HS, TQ : 2 * TQ] = zero
    w1[HS : 2 * HS, 0:TQ] = zero
    loads[0].wait()
    loads[1].wait()
    loads[2].wait()

    row = lax.broadcasted_iota(jnp.int32, (ROWS, TQ), 0)

    def first(i, carry):
        total, weighted = carry
        base = pl.multiple_of(i * ROWS, ROWS)
        both = jnp.dot(kv_v[pl.ds(base, ROWS), :], w1[...], preferred_element_type=F32)
        dprob = both[:, TQ:]
        pos = row + base
        allowed = jnp.logical_and(pos >= lo, pos < hi)
        expo = jnp.where(allowed, jnp.exp(both[:, :TQ]), 0.0)
        expo_s[pl.ds(base, ROWS), :] = expo
        dprob_s[pl.ds(base, ROWS), :] = dprob
        return total + fold8(expo), weighted + fold8(expo * dprob)

    zeros = jnp.zeros((8, TQ), F32)
    total, weighted = lax.fori_loop(0, S // ROWS, first, (zeros, zeros))
    total = jnp.sum(total, axis=0, keepdims=True)
    delta = jnp.sum(weighted, axis=0, keepdims=True) / total
    scale = 1.0 / total

    def second(i, _):
        base = pl.multiple_of(i * ROWS, ROWS)
        prob = expo_s[pl.ds(base, ROWS), :] * scale
        ds = (prob * (dprob_s[pl.ds(base, ROWS), :] - delta)).astype(BF16)
        ds_s[pl.ds(base, ROWS), :] = ds
        both = jnp.concatenate([ds, prob.astype(BF16)], axis=1)
        grads = lax.dot_general(both, w1[...], NT, preferred_element_type=F32).astype(BF16)
        msg[pl.ds(pl.multiple_of(i * (ROWS // OWN), ROWS // OWN), ROWS // OWN)] = grads.reshape(
            ROWS // OWN, OWN, 2 * HS
        )
        return 0

    lax.fori_loop(0, S // ROWS, second, 0)

    loads[3].wait()
    lr = lr_v[...].astype(F32)
    packed = jnp.concatenate([lr[8 * j : 8 * j + 8] for j in range(4)], axis=1).astype(BF16)
    lr_all[pl.ds(m, 1)] = packed.reshape(1, 8, 4 * RANK2)

    pl.semaphore_wait(barrier, MP - 1 + DP - self_adapter.astype(jnp.int32))

    for dz in Z_ORDER[:-1]:
        pltpu.make_async_remote_copy(
            src_ref=lr_all.at[m], dst_ref=lr_all.at[m], send_sem=lrz_send, recv_sem=lrz_recv,
            device_id=(p, peer_of(0, dz)), device_id_type=MESH,
        ).start()

    def send(first_one, last_one):
        for dx, dz in ORDER[first_one:last_one]:
            peer = peer_of(dx, dz)
            pltpu.make_async_remote_copy(
                src_ref=msg.at[peer], dst_ref=recv.at[m], send_sem=send_sem, recv_sem=recv_sem.at[dx],
                device_id=(p, peer), device_id_type=MESH,
            ).start()

    recv[pl.ds(m, 1)] = msg[pl.ds(m, 1)]
    send(0, 32)

    qg_out[...] = lax.dot_general(kv_v[...], ds_s[...], TN, preferred_element_type=F32)[:HS].astype(BF16)

    def wait_bytes(ref, count, sem):
        pltpu.make_async_copy(ref.at[pl.ds(0, count)], ref.at[pl.ds(0, count)], sem).wait()

    wait_bytes(lr_all, ZS - 1, lrz_recv)
    mine = lr_all.at[pl.ds(pl.multiple_of(x * ZS, ZS), ZS)]
    for j in (2, 1, 3):
        pltpu.make_async_remote_copy(
            src_ref=mine, dst_ref=mine, send_sem=lrx_send, recv_sem=lrx_recv,
            device_id=(p, peer_of(j, 0)), device_id_type=MESH,
        ).start()

    send(32, 46)

    wait_bytes(lr_all, ZS * (XS - 1), lrx_recv)
    gathered = lr_all[...].astype(F32)
    for j in range(4):
        lr_full[:, 8 * j : 8 * j + 8, :] = pltpu.roll(
            gathered.reshape(MP * 8, 4 * RANK2), (4 - j) % 4 * RANK2, axis=1
        ).reshape(MP, 8, 4 * RANK2)
    terms = lax.dot_general(
        msg[...].reshape(S, 2 * HS), lr_full[...].reshape(S, 4 * RANK2).astype(BF16), TN,
        preferred_element_type=F32,
    )
    lane = lax.broadcasted_iota(jnp.int32, (HS, 4 * RANK2), 1)
    term_s[...] = jnp.where(lane < RANK2 // 2, terms[:HS], terms[HS:])
    group = lax.broadcasted_iota(jnp.int32, (HS // 4, 4 * RANK2), 1) // RANK2
    full = term_s[pl.ds(0, HS // 4, stride=4), :]
    for j in range(1, 4):
        full = jnp.where(
            group == j, pltpu.roll(term_s[pl.ds(j, HS // 4, stride=4), :], j * RANK2, axis=1), full
        )
    for k in range(8):
        adapter_send[k] = full[2 * k : 2 * k + 2]

    send(46, 54)

    for k in range(8):
        dst_mp = 8 * gb + k
        me = jnp.logical_and(p == ga, dst_mp == m)

        @pl.when(jnp.logical_not(me))
        def _():
            pltpu.make_async_remote_copy(
                src_ref=adapter_send.at[k], dst_ref=adapter_recv.at[p], send_sem=ad_send, recv_sem=ad_recv,
                device_id=(ga, dst_mp), device_id_type=MESH,
            ).start()

        @pl.when(me)
        def _():
            pltpu.make_async_copy(adapter_send.at[k], adapter_recv.at[p], own_sem).start()

    send(54, MP - 1)

    loads[4].wait()

    def place(dx):
        wait_bytes(recv, ZS if dx else ZS - 1, recv_sem.at[dx])
        column = lax.rem(x + XS - dx, XS)
        for j in range(ZS // 2):
            a = recv[column * ZS + 2 * j]
            b = recv[column * ZS + 2 * j + 1]
            lanes = pl.ds(pl.multiple_of(column * (ZS * HS) + 128 * j, 128), 128)
            grads[0:OWN, lanes] = jnp.concatenate([a[:, :HS], b[:, :HS]], axis=1)
            grads[OWN : 2 * OWN, lanes] = jnp.concatenate([a[:, HS:], b[:, HS:]], axis=1)
        lanes = pl.ds(pl.multiple_of(column * (ZS * HS), ZS * HS), ZS * HS)
        return lax.dot_general(grads[:, lanes], up[:, lanes], NT, preferred_element_type=F32)

    both = place(2)
    both = both + place(1)
    both = both + place(3)

    wait_bytes(lr_all, ZS - 1, lrz_send)
    wait_bytes(lr_all, ZS * (XS - 1), lrx_send)

    @pl.when(self_adapter)
    def _():
        wait_bytes(adapter_send, 1, own_sem)
        wait_bytes(adapter_send, 7, ad_send)
        wait_bytes(adapter_recv, 7, ad_recv)

    @pl.when(jnp.logical_not(self_adapter))
    def _():
        wait_bytes(adapter_send, 8, ad_send)
        wait_bytes(adapter_recv, 8, ad_recv)

    total = ADAPTER_FACTOR * jnp.sum(adapter_recv[...], axis=0)
    for r in range(8):
        aug_out[r : r + 1, :] = total[r // 4 : r // 4 + 1, r % 4 * RANK2 : (r % 4 + 1) * RANK2]

    wait_bytes(msg, MP - 1, send_sem)
    both = both + place(0)
    lane = lax.broadcasted_iota(jnp.int32, (OWN, RANK2), 1)
    lrg_out[...] = ADAPTER_FACTOR * jnp.where(lane < RANK2 // 2, both[:OWN], both[OWN:])


def leave_kernel(grads, lrg, aug, qg, key_out, value_out, lrg_out, aug_out, qg_out, sem):
    copies = [
        pltpu.make_async_copy(a, b, sem.at[i])
        for i, (a, b) in enumerate(
            (
                (grads.at[0:OWN], key_out),
                (grads.at[OWN : 2 * OWN], value_out),
                (lrg, lrg_out),
                (aug, aug_out),
                (qg, qg_out),
            )
        )
    ]
    for copy in copies:
        copy.start()
    for copy in copies:
        copy.wait()


def local(query, kv_cache, out_grad, source_lengths, target_lengths, low_rank, adapter_up_matrix):
    any_spec = pl.BlockSpec(memory_space=pl.ANY)
    vmem = pl.BlockSpec(memory_space=pltpu.VMEM)
    inside = pl.pallas_call(
        exchange_kernel,
        out_shape=(
            pltpu.VMEM((2 * OWN, MP * HS), BF16),
            pltpu.VMEM((OWN, RANK2), F32),
            pltpu.VMEM((8, RANK2), F32),
            pltpu.VMEM((HS, TQ), BF16),
        ),
        in_specs=[any_spec] * 7,
        out_specs=(vmem,) * 4,
        scratch_shapes=[
            pltpu.SMEM((1, NDOC), jnp.int32),
            pltpu.SMEM((1, NDOC), jnp.int32),
            pltpu.VMEM((S, 2 * HS), BF16),
            pltpu.VMEM((OWN, RANK2), BF16),
            pltpu.VMEM((RANK2, MP * HS), BF16),
            pltpu.VMEM((2 * HS, 2 * TQ), BF16),
            pltpu.VMEM((S, TQ), F32),
            pltpu.VMEM((S, TQ), F32),
            pltpu.VMEM((S, TQ), BF16),
            pltpu.VMEM((MP, OWN, 2 * HS), BF16),
            pltpu.VMEM((MP, 8, 4 * RANK2), BF16),
            pltpu.VMEM((MP, OWN, 4 * RANK2), F32),
            pltpu.VMEM((HS, 4 * RANK2), F32),
            pltpu.VMEM((8, 2, 4 * RANK2), F32),
            pltpu.VMEM((MP, OWN, 2 * HS), BF16),
            pltpu.VMEM((DP, 2, 4 * RANK2), F32),
            pltpu.SemaphoreType.DMA((7,)),
            pltpu.SemaphoreType.DMA,
            pltpu.SemaphoreType.DMA((XS,)),
            pltpu.SemaphoreType.DMA,
            pltpu.SemaphoreType.DMA,
            pltpu.SemaphoreType.DMA,
            pltpu.SemaphoreType.DMA,
            pltpu.SemaphoreType.DMA,
            pltpu.SemaphoreType.DMA,
            pltpu.SemaphoreType.DMA,
        ],
        compiler_params=pltpu.CompilerParams(
            collective_id=0, has_side_effects=True, vmem_limit_bytes=VMEM_LIMIT
        ),
        name="exchange",
    )(query.T, kv_cache, out_grad.T, source_lengths, target_lengths, low_rank, adapter_up_matrix)
    inside = [pltpu.with_memory_space_constraint(a, pltpu.VMEM) for a in inside]
    key_gradient, value_grad, low_rank_gradient, adapter_up_gradient, query_grad = pl.pallas_call(
        leave_kernel,
        out_shape=(
            jax.ShapeDtypeStruct((OWN, MP * HS), BF16),
            jax.ShapeDtypeStruct((OWN, MP * HS), BF16),
            jax.ShapeDtypeStruct((OWN, RANK2), F32),
            jax.ShapeDtypeStruct((8, RANK2), F32),
            jax.ShapeDtypeStruct((HS, TQ), BF16),
        ),
        in_specs=[vmem] * 4,
        out_specs=(any_spec,) * 5,
        scratch_shapes=[pltpu.SemaphoreType.DMA((5,))],
        compiler_params=pltpu.CompilerParams(vmem_limit_bytes=LEAVE_VMEM),
        name="leave",
    )(*inside)
    return query_grad.T, key_gradient, value_grad, low_rank_gradient, adapter_up_gradient


def solution(mesh):
    in_specs = (
        P("dp", "mp"),
        P("dp", "mp"),
        P("dp", "mp"),
        P("dp", None),
        P("dp", None),
        P(("dp", "mp"), None),
        P(),
    )
    out_specs = (
        P("dp", "mp"),
        P(("dp", "mp"), None),
        P(("dp", "mp"), None),
        P(("dp", "mp"), None),
        P(("dp", "mp"), None),
    )
    return jax.shard_map(local, mesh=mesh, in_specs=in_specs, out_specs=out_specs, check_vma=False)
```

```python
import functools

import jax
import jax.numpy as jnp
from jax import lax
from jax.experimental import pallas as pl
from jax.experimental.pallas import tpu as pltpu
from jax.sharding import PartitionSpec as P

HS = 64
XS, ZS = 4, 16
MP = XS * ZS
DP = 8
NDOC = 8
TQ = 256
S = 2048
OWN = S // MP
RANK2 = 32
ROWS = 256
ADAPTER_FACTOR = 2.0
VMEM_LIMIT = 67_043_328 - (720 << 10)
LEAVE_VMEM = 67_043_328 - (720 << 10)
MESH = pl.DeviceIdType.MESH
F32 = jnp.float32
BF16 = jnp.bfloat16
NT = (((1,), (1,)), ((), ()))
TN = (((0,), (0,)), ((), ()))


def fold8(x):
    return jnp.sum(x.reshape(x.shape[0] // 8, 8, x.shape[1]), axis=0)


Z_ORDER = (8, 1, 15, 7, 9, 2, 14, 6, 10, 3, 13, 5, 11, 4, 12, 0)
ORDER = [(dx, dz) for dx in (2, 1, 3, 0) for dz in Z_ORDER if (dx, dz) != (0, 0)]


def exchange_kernel(
    q_hbm, kv_hbm, g_hbm, slen_hbm, tlen_hbm, lr_hbm, up_hbm,
    grads, lrg_out, aug_out, qg_out,
    slen, tlen, kv_v, lr_v, up, w1, expo_s, dprob_s, ds_s, msg, msg_t, lr_all, lr_full, term_s, adapter_send, recv, adapter_recv,
    in_sem, send_sem, recv_sem, lrz_send, lrz_recv, lrx_send, lrx_recv, ad_send, ad_recv, own_sem,
):
    p = lax.axis_index("dp")
    m = lax.axis_index("mp")
    x = lax.div(m, ZS)
    z = lax.rem(m, ZS)
    ga = lax.div(m, 8)
    gb = lax.rem(m, 8)
    self_adapter = jnp.logical_and(p == ga, gb == ga)

    barrier = pltpu.get_barrier_semaphore()

    def peer_of(dx, dz):
        return lax.rem(x + dx, XS) * ZS + lax.rem(z + dz, ZS)

    for dx, dz in ORDER:
        pl.semaphore_signal(barrier, inc=1, device_id=(p, peer_of(dx, dz)), device_id_type=MESH)
    src_head = 8 * p + ga
    for j in range(DP):
        not_me = jnp.logical_not(jnp.logical_and(p == j, src_head == m))

        @pl.when(not_me)
        def _():
            pl.semaphore_signal(barrier, inc=1, device_id=(j, src_head), device_id_type=MESH)

    loads = [
        pltpu.make_async_copy(a, b, in_sem.at[i])
        for i, (a, b) in enumerate(
            (
                (q_hbm, w1.at[0:HS, 0:TQ]),
                (g_hbm, w1.at[HS : 2 * HS, TQ : 2 * TQ]),
                (kv_hbm, kv_v),
                (lr_hbm, lr_v),
                (up_hbm, up),
                (slen_hbm, slen),
                (tlen_hbm, tlen),
            )
        )
    ]
    for c in loads:
        c.start()

    loads[5].wait()
    loads[6].wait()
    col = lax.broadcasted_iota(jnp.int32, (8, TQ), 1)
    lo = jnp.zeros((8, TQ), jnp.int32)
    hi = jnp.zeros((8, TQ), jnp.int32)
    start = jnp.int32(0)
    for k in range(NDOC):
        width = slen[0, k]
        hi = hi + jnp.where(col >= start, width, 0)
        start = start + tlen[0, k]
        lo = lo + jnp.where(col >= start, width, 0)
    lo = lo[0:1]
    hi = hi[0:1]

    zero = jnp.zeros((HS, TQ), BF16)
    w1[0:HS, TQ : 2 * TQ] = zero
    w1[HS : 2 * HS, 0:TQ] = zero
    loads[0].wait()
    loads[1].wait()
    loads[2].wait()

    row = lax.broadcasted_iota(jnp.int32, (ROWS, TQ), 0)

    def first(i, carry):
        total, weighted = carry
        base = pl.multiple_of(i * ROWS, ROWS)
        both = jnp.dot(kv_v[pl.ds(base, ROWS), :], w1[...], preferred_element_type=F32)
        dprob = both[:, TQ:]
        pos = row + base
        allowed = jnp.logical_and(pos >= lo, pos < hi)
        expo = jnp.where(allowed, jnp.exp(both[:, :TQ]), 0.0)
        expo_s[pl.ds(base, ROWS), :] = expo
        dprob_s[pl.ds(base, ROWS), :] = dprob
        return total + fold8(expo), weighted + fold8(expo * dprob)

    zeros = jnp.zeros((8, TQ), F32)
    total, weighted = lax.fori_loop(0, S // ROWS, first, (zeros, zeros))
    total = jnp.sum(total, axis=0, keepdims=True)
    delta = jnp.sum(weighted, axis=0, keepdims=True) / total
    scale = 1.0 / total

    def second(i, _):
        base = pl.multiple_of(i * ROWS, ROWS)
        prob = expo_s[pl.ds(base, ROWS), :] * scale
        ds = (prob * (dprob_s[pl.ds(base, ROWS), :] - delta)).astype(BF16)
        ds_s[pl.ds(base, ROWS), :] = ds
        both = jnp.concatenate([ds, prob.astype(BF16)], axis=1)
        grads = lax.dot_general(both, w1[...], NT, preferred_element_type=F32).astype(BF16)
        msg[pl.ds(pl.multiple_of(i * (ROWS // OWN), ROWS // OWN), ROWS // OWN)] = grads.reshape(
            ROWS // OWN, OWN, 2 * HS
        )
        return 0

    lax.fori_loop(0, S // ROWS, second, 0)

    loads[3].wait()
    lr = lr_v[...].astype(F32)
    packed = jnp.concatenate([lr[8 * j : 8 * j + 8] for j in range(4)], axis=1).astype(BF16)
    lr_all[pl.ds(m, 1)] = packed.reshape(1, 8, 4 * RANK2)

    pl.semaphore_wait(barrier, MP - 1 + DP - self_adapter.astype(jnp.int32))

    for dz in Z_ORDER[:-1]:
        pltpu.make_async_remote_copy(
            src_ref=lr_all.at[m], dst_ref=lr_all.at[m], send_sem=lrz_send, recv_sem=lrz_recv,
            device_id=(p, peer_of(0, dz)), device_id_type=MESH,
        ).start()

    def send(first_one, last_one):
        for dx, dz in ORDER[first_one:last_one]:
            peer = peer_of(dx, dz)
            pltpu.make_async_remote_copy(
                src_ref=msg.at[peer], dst_ref=recv.at[m], send_sem=send_sem, recv_sem=recv_sem.at[dx],
                device_id=(p, peer), device_id_type=MESH,
            ).start()

    recv[pl.ds(m, 1)] = msg[pl.ds(m, 1)]
    send(0, 32)

    qg_out[...] = lax.dot_general(kv_v[...], ds_s[...], TN, preferred_element_type=F32)[:HS].astype(BF16)

    def wait_bytes(ref, count, sem):
        pltpu.make_async_copy(ref.at[pl.ds(0, count)], ref.at[pl.ds(0, count)], sem).wait()

    msg_t[...] = msg[...].reshape(S, 2 * HS).T

    wait_bytes(lr_all, ZS - 1, lrz_recv)
    mine = lr_all.at[pl.ds(pl.multiple_of(x * ZS, ZS), ZS)]
    for j in (2, 1, 3):
        pltpu.make_async_remote_copy(
            src_ref=mine, dst_ref=mine, send_sem=lrx_send, recv_sem=lrx_recv,
            device_id=(p, peer_of(j, 0)), device_id_type=MESH,
        ).start()

    send(32, 46)

    wait_bytes(lr_all, ZS * (XS - 1), lrx_recv)
    gathered = lr_all[...].astype(F32)
    for j in range(4):
        lr_full[:, 8 * j : 8 * j + 8, :] = pltpu.roll(
            gathered.reshape(MP * 8, 4 * RANK2), (4 - j) % 4 * RANK2, axis=1
        ).reshape(MP, 8, 4 * RANK2)
    terms = jnp.dot(
        msg_t[...], lr_full[...].reshape(S, 4 * RANK2).astype(BF16), preferred_element_type=F32
    )
    lane = lax.broadcasted_iota(jnp.int32, (HS, 4 * RANK2), 1)
    term_s[...] = jnp.where(lane < RANK2 // 2, terms[:HS], terms[HS:])
    group = lax.broadcasted_iota(jnp.int32, (HS // 4, 4 * RANK2), 1) // RANK2
    full = term_s[pl.ds(0, HS // 4, stride=4), :]
    for j in range(1, 4):
        full = jnp.where(
            group == j, pltpu.roll(term_s[pl.ds(j, HS // 4, stride=4), :], j * RANK2, axis=1), full
        )
    for k in range(8):
        adapter_send[k] = full[2 * k : 2 * k + 2]

    send(46, 54)

    for k in range(8):
        dst_mp = 8 * gb + k
        me = jnp.logical_and(p == ga, dst_mp == m)

        @pl.when(jnp.logical_not(me))
        def _():
            pltpu.make_async_remote_copy(
                src_ref=adapter_send.at[k], dst_ref=adapter_recv.at[p], send_sem=ad_send, recv_sem=ad_recv,
                device_id=(ga, dst_mp), device_id_type=MESH,
            ).start()

        @pl.when(me)
        def _():
            pltpu.make_async_copy(adapter_send.at[k], adapter_recv.at[p], own_sem).start()

    send(54, MP - 1)

    loads[4].wait()

    def place(dx):
        wait_bytes(recv, ZS if dx else ZS - 1, recv_sem.at[dx])
        column = lax.rem(x + XS - dx, XS)
        for j in range(ZS // 2):
            a = recv[column * ZS + 2 * j]
            b = recv[column * ZS + 2 * j + 1]
            lanes = pl.ds(pl.multiple_of(column * (ZS * HS) + 128 * j, 128), 128)
            grads[0:OWN, lanes] = jnp.concatenate([a[:, :HS], b[:, :HS]], axis=1)
            grads[OWN : 2 * OWN, lanes] = jnp.concatenate([a[:, HS:], b[:, HS:]], axis=1)
        lanes = pl.ds(pl.multiple_of(column * (ZS * HS), ZS * HS), ZS * HS)
        return lax.dot_general(grads[:, lanes], up[:, lanes], NT, preferred_element_type=F32)

    both = place(2)
    both = both + place(1)
    both = both + place(3)

    wait_bytes(lr_all, ZS - 1, lrz_send)
    wait_bytes(lr_all, ZS * (XS - 1), lrx_send)

    @pl.when(self_adapter)
    def _():
        wait_bytes(adapter_send, 1, own_sem)
        wait_bytes(adapter_send, 7, ad_send)
        wait_bytes(adapter_recv, 7, ad_recv)

    @pl.when(jnp.logical_not(self_adapter))
    def _():
        wait_bytes(adapter_send, 8, ad_send)
        wait_bytes(adapter_recv, 8, ad_recv)

    total = ADAPTER_FACTOR * jnp.sum(adapter_recv[...], axis=0)
    for r in range(8):
        aug_out[r : r + 1, :] = total[r // 4 : r // 4 + 1, r % 4 * RANK2 : (r % 4 + 1) * RANK2]

    wait_bytes(msg, MP - 1, send_sem)
    both = both + place(0)
    lane = lax.broadcasted_iota(jnp.int32, (OWN, RANK2), 1)
    lrg_out[...] = ADAPTER_FACTOR * jnp.where(lane < RANK2 // 2, both[:OWN], both[OWN:])


def leave_kernel(grads, lrg, aug, qg, key_out, value_out, lrg_out, aug_out, qg_out, sem):
    copies = [
        pltpu.make_async_copy(a, b, sem.at[i])
        for i, (a, b) in enumerate(
            (
                (grads.at[0:OWN], key_out),
                (grads.at[OWN : 2 * OWN], value_out),
                (lrg, lrg_out),
                (aug, aug_out),
                (qg, qg_out),
            )
        )
    ]
    for copy in copies:
        copy.start()
    for copy in copies:
        copy.wait()


def local(query, kv_cache, out_grad, source_lengths, target_lengths, low_rank, adapter_up_matrix):
    any_spec = pl.BlockSpec(memory_space=pl.ANY)
    vmem = pl.BlockSpec(memory_space=pltpu.VMEM)
    inside = pl.pallas_call(
        exchange_kernel,
        out_shape=(
            pltpu.VMEM((2 * OWN, MP * HS), BF16),
            pltpu.VMEM((OWN, RANK2), F32),
            pltpu.VMEM((8, RANK2), F32),
            pltpu.VMEM((HS, TQ), BF16),
        ),
        in_specs=[any_spec] * 7,
        out_specs=(vmem,) * 4,
        scratch_shapes=[
            pltpu.SMEM((1, NDOC), jnp.int32),
            pltpu.SMEM((1, NDOC), jnp.int32),
            pltpu.VMEM((S, 2 * HS), BF16),
            pltpu.VMEM((OWN, RANK2), BF16),
            pltpu.VMEM((RANK2, MP * HS), BF16),
            pltpu.VMEM((2 * HS, 2 * TQ), BF16),
            pltpu.VMEM((S, TQ), F32),
            pltpu.VMEM((S, TQ), F32),
            pltpu.VMEM((S, TQ), BF16),
            pltpu.VMEM((MP, OWN, 2 * HS), BF16),
            pltpu.VMEM((2 * HS, S), BF16),
            pltpu.VMEM((MP, 8, 4 * RANK2), BF16),
            pltpu.VMEM((MP, OWN, 4 * RANK2), F32),
            pltpu.VMEM((HS, 4 * RANK2), F32),
            pltpu.VMEM((8, 2, 4 * RANK2), F32),
            pltpu.VMEM((MP, OWN, 2 * HS), BF16),
            pltpu.VMEM((DP, 2, 4 * RANK2), F32),
            pltpu.SemaphoreType.DMA((7,)),
            pltpu.SemaphoreType.DMA,
            pltpu.SemaphoreType.DMA((XS,)),
            pltpu.SemaphoreType.DMA,
            pltpu.SemaphoreType.DMA,
            pltpu.SemaphoreType.DMA,
            pltpu.SemaphoreType.DMA,
            pltpu.SemaphoreType.DMA,
            pltpu.SemaphoreType.DMA,
            pltpu.SemaphoreType.DMA,
        ],
        compiler_params=pltpu.CompilerParams(
            collective_id=0, has_side_effects=True, vmem_limit_bytes=VMEM_LIMIT
        ),
        name="exchange",
    )(query.T, kv_cache, out_grad.T, source_lengths, target_lengths, low_rank, adapter_up_matrix)
    inside = [pltpu.with_memory_space_constraint(a, pltpu.VMEM) for a in inside]
    key_gradient, value_grad, low_rank_gradient, adapter_up_gradient, query_grad = pl.pallas_call(
        leave_kernel,
        out_shape=(
            jax.ShapeDtypeStruct((OWN, MP * HS), BF16),
            jax.ShapeDtypeStruct((OWN, MP * HS), BF16),
            jax.ShapeDtypeStruct((OWN, RANK2), F32),
            jax.ShapeDtypeStruct((8, RANK2), F32),
            jax.ShapeDtypeStruct((HS, TQ), BF16),
        ),
        in_specs=[vmem] * 4,
        out_specs=(any_spec,) * 5,
        scratch_shapes=[pltpu.SemaphoreType.DMA((5,))],
        compiler_params=pltpu.CompilerParams(vmem_limit_bytes=LEAVE_VMEM),
        name="leave",
    )(*inside)
    return query_grad.T, key_gradient, value_grad, low_rank_gradient, adapter_up_gradient


def solution(mesh):
    in_specs = (
        P("dp", "mp"),
        P("dp", "mp"),
        P("dp", "mp"),
        P("dp", None),
        P("dp", None),
        P(("dp", "mp"), None),
        P(),
    )
    out_specs = (
        P("dp", "mp"),
        P(("dp", "mp"), None),
        P(("dp", "mp"), None),
        P(("dp", "mp"), None),
        P(("dp", "mp"), None),
    )
    return jax.shard_map(local, mesh=mesh, in_specs=in_specs, out_specs=out_specs, check_vma=False)
```
